32 devices in a mesh: dp: 8 (over z, x), mp: 4 (over y, core).
Axes of the slice: x: 2, y: 2, z: 4, core: 2. Of those that a mesh axis runs over, the one named last changes fastest.
Arguments:
- tokens: bfloat16 [4096, 768], P(('dp', 'mp')), may hold values from -6 to 6
- cotangent: bfloat16 [4096, 768], P(('dp', 'mp')), may hold values from -6 to 6
- attn_gain: bfloat16 [768], P('dp'), may hold values from 0.25 to 1.75
- w_qkv: bfloat16 [768, 3, 768], P('dp', None, 'mp'), as said below
- w_attn_out: bfloat16 [768, 768], P('mp', 'dp'), may hold values from -2.5 to 2.5
- mlp_gain: bfloat16 [768], P('dp'), may hold values from 0.25 to 1.75
- w_in: bfloat16 [768, 2, 1152], P('dp', None, 'mp'), may hold values from -0.21875 to 0.21875
- w_mlp_out: bfloat16 [1152, 768], P('mp', 'dp'), may hold values from -0.1875 to 0.1875
Outputs:
- output: float32 [4096, 768], P(('dp', 'mp'))
- tokens_grad: float32 [4096, 768], P(('dp', 'mp'))
- attn_gain_grad: float32 [768], P('dp')
- w_qkv_grad: float32 [768, 3, 768], P('dp', None, 'mp')
- w_attn_out_grad: float32 [768, 768], P('mp', 'dp')
- mlp_gain_grad: float32 [768], P('dp')
- w_in_grad: float32 [768, 2, 1152], P('dp', None, 'mp')
- w_mlp_out_grad: float32 [1152, 768], P('mp', 'dp')
The draws below stay inside these ranges and needn't reach their ends.
Inputs may be any that keep to these rules, and one draw needn't show every extreme that they name: Entries of w_qkv lie within plus or minus 8 / sqrt(768).
All inputs are finite; a program needn't handle non-finite values.
Results may differ from the reference program's by a relative error of at most 0.015.
Values may be sent and summed in bfloat16 or wider, within the bound.
A program may use at most 64 MiB of HBM per device.

```python
import jax
import jax.numpy as jnp
from jax import lax

D = 768
HEADS = 12
FF = 1152
HEAD_DIM = 64
SEQ_LEN = 512
TOKENS = 4096
N_DP = 8


def draw_w_qkv(key, part):
    values = jnp.clip(jax.random.normal(key, (D, 3, D), jnp.float32), -8.0, 8.0)
    return (values * D ** (-0.5)).astype(jnp.bfloat16)


def raised(values, rng, source, target, blocks, factor):
    owner, partner = [(jnp.arange(values.shape[dim]) // (values.shape[dim] // blocks)).reshape([-1 if axis == dim else 1 for axis in range(values.ndim)]) for dim in (source, target)]
    chosen = jax.random.permutation(rng, blocks)[partner]
    strong = (owner == chosen) | (owner == (partner + blocks // 2) % blocks)
    return jnp.where(strong, factor * values, values)


def levels(rng, shape, shards, least, largest):
    factor_of, own = 1.0, jax.random.fold_in(rng, 6)
    for axis_at, blocks in shards:
        heights = jnp.exp(jax.random.uniform(jax.random.fold_in(own, axis_at), (blocks,), jnp.float32, least / len(shards), largest / len(shards)))
        factor_of = factor_of * jnp.repeat(heights, shape[axis_at] // blocks).reshape([-1 if axis == axis_at else 1 for axis in range(len(shape))])
    return factor_of


def centred(key, extent, scale, bound, split=(), held_as=jnp.bfloat16):
    factor_of = levels(key, extent, split, -0.22, 0.18) if split else 1.0
    result = jax.random.normal(key, extent, jnp.float32) * scale * factor_of
    return jnp.minimum(jnp.maximum(result, -bound), bound).astype(held_as)


def heavy_noise(rng, shape, spread, most, shards, heavy, kind=jnp.bfloat16):
    entries = spread * jax.random.normal(rng, shape, jnp.float32)
    if shards:
        entries = entries * levels(rng, shape, shards, -0.22, 0.18)
    return jnp.clip(raised(entries, jax.random.fold_in(rng, 3), *heavy), -most, most).astype(kind)


def setup_inputs(seed: int = 0) -> dict:
    key_of = jax.random.split(jax.random.key(seed), 9)
    return {
        "tokens": heavy_noise(key_of[0], (TOKENS, D), 1.0, 6.0, ((0, 32),), (0, 1, 32, 2.75)),
        "cotangent": heavy_noise(key_of[1], (TOKENS, D), 1.0, 6.0, ((0, 32),), (0, 1, 32, 2.75)),
        "attn_gain": jnp.clip(1.0 + 0.15 * jax.random.normal(key_of[2], (D,), jnp.float32), 0.25, 1.75).astype(jnp.bfloat16),
        "w_qkv": draw_w_qkv(jax.random.fold_in(key_of[8], 71), 0),
        "w_attn_out": centred(key_of[4], (D, D), (max(1, D * 4 // SEQ_LEN)) ** -0.5, 2.5, ((0, 4), (1, 8))),
        "mlp_gain": jnp.clip(1.0 + 0.15 * jax.random.normal(key_of[5], (D,), jnp.float32), 0.25, 1.75).astype(jnp.bfloat16),
        "w_in": centred(key_of[6], (D, 2, FF), D ** -0.5, 0.21875, ((0, 8), (2, 4))),
        "w_mlp_out": centred(key_of[7], (FF, D), FF ** -0.5, 0.1875, ((0, 4), (1, 8))),
    }


norm_eps = 1e-05
rope_base = 160000.0
query_block = 512

def rotary_tables(length, head_width):
    half_width = head_width // 2
    freqs = rope_base ** (-(jnp.arange(half_width, dtype=jnp.float32) * 2.0 / head_width))
    angles = jnp.arange(length, dtype=jnp.float32)[:, None] * freqs[None, :]
    angles = jnp.concatenate([angles, angles], axis=1)
    return (jnp.cos(angles), jnp.sin(angles))

def rotate_half(values):
    half_width = values.shape[-1] // 2
    return jnp.concatenate([-values[..., half_width:], values[..., :half_width]], axis=-1)

def apply_rotary(values, cosine_table, sine_table):
    return values * cosine_table[:, None, :] + rotate_half(values) * sine_table[:, None, :]

def undo_rotary(grads, cosine_table, sine_table):
    return grads * cosine_table[:, None, :] - rotate_half(grads * sine_table[:, None, :])

def norm_stats(values):
    centered = values - lax.optimization_barrier(jnp.mean(values, axis=-1, keepdims=True))
    variance = lax.optimization_barrier(jnp.mean(centered * centered, axis=-1, keepdims=True))
    inverse = lax.rsqrt(variance + norm_eps)
    return (centered * inverse, inverse)

def norm_backward(grad_out, normed, inverse, gain_vals):
    scaled = grad_out * gain_vals
    grad_in = inverse * (scaled - lax.optimization_barrier(jnp.mean(scaled, axis=-1, keepdims=True)) - normed * lax.optimization_barrier(jnp.mean(scaled * normed, axis=-1, keepdims=True)))
    return (grad_in, lax.optimization_barrier(jnp.sum(grad_out * normed, axis=0)))

def gelu_exact(values):
    return 0.5 * values * (1.0 + jax.scipy.special.erf(values * 0.7071067811865476))

def gelu_slope(values):
    return 0.5 * (1.0 + jax.scipy.special.erf(values * 0.7071067811865476)) + values * jnp.exp(-0.5 * values * values) * 0.3989422804014327

def mixing(form, left, right):
    return jnp.einsum(form, left.astype(jnp.float32), right.astype(jnp.float32))

def attention_forward(queries, key_rows, value_rows):
    length, head_count, head_width = queries.shape
    block_size = min(query_block, length)
    score_scale = head_width ** (-0.5)
    blocks = queries.reshape(length // block_size, block_size, head_count, head_width)

    def one_block(block_rows):
        scores = mixing('qhd,khd->hqk', block_rows, key_rows) * score_scale
        row_peak = lax.optimization_barrier(jnp.max(scores, axis=-1, keepdims=True))
        exp_scores = jnp.exp(scores - row_peak)
        row_total = lax.optimization_barrier(jnp.sum(exp_scores, axis=-1, keepdims=True))
        attn_probs = (exp_scores / row_total).astype(jnp.bfloat16)
        block_out = mixing('hqk,khd->qhd', attn_probs, value_rows)
        return (block_out.astype(jnp.bfloat16), (row_peak + jnp.log(row_total))[..., 0])
    outs, log_totals = lax.map(one_block, blocks)
    return (outs.reshape(length, head_count, head_width), log_totals)

def attention_backward(queries, key_rows, value_rows, attended, log_totals, grad_out):
    length, head_count, head_width = queries.shape
    block_size = min(query_block, length)
    nblocks = length // block_size
    score_scale = head_width ** (-0.5)

    def one_block(running, block_inputs):
        key_grad, value_grad = running
        block_rows, out_rows, grad_rows, lse_rows = block_inputs
        scores = mixing('qhd,khd->hqk', block_rows, key_rows) * score_scale
        attn_probs = jnp.exp(scores - lse_rows[..., None])
        value_grad = value_grad + mixing('hqk,qhd->khd', attn_probs.astype(jnp.bfloat16), grad_rows)
        dprobs = mixing('qhd,khd->hqk', grad_rows, value_rows)
        row_delta = lax.optimization_barrier(jnp.sum(grad_rows.astype(jnp.float32) * out_rows.astype(jnp.float32), axis=-1)).T
        dscores = (attn_probs * (dprobs - row_delta[..., None]) * score_scale).astype(jnp.bfloat16)
        query_grad = mixing('hqk,khd->qhd', dscores, key_rows)
        key_grad = key_grad + mixing('hqk,qhd->khd', dscores, block_rows)
        return ((key_grad, value_grad), query_grad)
    zero_grad = jnp.zeros((length, head_count, head_width), jnp.float32)
    shape_blocks = (nblocks, block_size, head_count, head_width)
    block_inputs = (queries.reshape(shape_blocks), attended.reshape(shape_blocks), grad_out.reshape(shape_blocks), log_totals)
    (key_grad, value_grad), query_grad = lax.scan(one_block, (zero_grad, zero_grad), block_inputs)
    return (query_grad.reshape(length, head_count, head_width), key_grad, value_grad)

def one_sequence(seq_rows, seq_cot, attn_gain, w_qkv, w_attn_out, mlp_gain, w_in, w_mlp_out):
    length = seq_rows.shape[0]
    cosine_table, sine_table = rotary_tables(length, HEAD_DIM)
    residual = seq_rows.astype(jnp.float32)
    normed_one, inverse_one = norm_stats(residual)
    first_in = (normed_one * attn_gain.astype(jnp.float32)).astype(jnp.bfloat16)
    qkv_flat = w_qkv.reshape(D, 3 * D)
    projected = jnp.dot(first_in, qkv_flat, preferred_element_type=jnp.float32).reshape(length, 3, HEADS, HEAD_DIM)
    queries = apply_rotary(projected[:, 0], cosine_table, sine_table).astype(jnp.bfloat16)
    key_rows = apply_rotary(projected[:, 1], cosine_table, sine_table).astype(jnp.bfloat16)
    value_rows = projected[:, 2].astype(jnp.bfloat16)
    attended, log_totals = attention_forward(queries, key_rows, value_rows)
    attended_flat = attended.reshape(length, D)
    mixed_rows = residual + jnp.dot(attended_flat, w_attn_out, preferred_element_type=jnp.float32)
    normed_two, inverse_two = norm_stats(mixed_rows)
    second_in = (normed_two * mlp_gain.astype(jnp.float32)).astype(jnp.bfloat16)
    in_flat = w_in.reshape(D, 2 * FF)
    lifted = jnp.dot(second_in, in_flat, preferred_element_type=jnp.float32).reshape(length, 2, FF)
    inputs = lifted[:, 0]
    gate_vals = lifted[:, 1]
    activated = gelu_exact(inputs)
    hidden = (activated * gate_vals).astype(jnp.bfloat16)
    output = mixed_rows + jnp.dot(hidden, w_mlp_out, preferred_element_type=jnp.float32)
    hidden_grad = jnp.dot(seq_cot, w_mlp_out.T, preferred_element_type=jnp.float32)
    down_grad = jnp.dot(hidden.T, seq_cot, preferred_element_type=jnp.float32)
    input_grad = hidden_grad * gate_vals * gelu_slope(inputs)
    gate_grad = hidden_grad * activated
    lifted_grad = jnp.stack([input_grad, gate_grad], axis=1).astype(jnp.bfloat16).reshape(length, 2 * FF)
    in_grad = jnp.dot(second_in.T, lifted_grad, preferred_element_type=jnp.float32).reshape(D, 2, FF)
    second_grad = jnp.dot(lifted_grad, in_flat.T, preferred_element_type=jnp.float32)
    back_two, gain_two_grad = norm_backward(second_grad, normed_two, inverse_two, mlp_gain.astype(jnp.float32))
    mixed_grad = seq_cot.astype(jnp.float32) + back_two
    mixed_low = mixed_grad.astype(jnp.bfloat16)
    attended_grad = jnp.dot(mixed_low, w_attn_out.T, preferred_element_type=jnp.float32).astype(jnp.bfloat16).reshape(length, HEADS, HEAD_DIM)
    out_grad = jnp.dot(attended_flat.T, mixed_low, preferred_element_type=jnp.float32)
    query_grad, key_grad, value_grad = attention_backward(queries, key_rows, value_rows, attended, log_totals, attended_grad)
    query_grad = undo_rotary(query_grad, cosine_table, sine_table)
    key_grad = undo_rotary(key_grad, cosine_table, sine_table)
    projected_grad = jnp.stack([query_grad, key_grad, value_grad], axis=1).astype(jnp.bfloat16).reshape(length, 3 * D)
    qkv_grad = jnp.dot(first_in.T, projected_grad, preferred_element_type=jnp.float32).reshape(D, 3, D)
    first_grad = jnp.dot(projected_grad, qkv_flat.T, preferred_element_type=jnp.float32)
    back_one, gain_one_grad = norm_backward(first_grad, normed_one, inverse_one, attn_gain.astype(jnp.float32))
    tokens_grad = mixed_grad + back_one
    return (output, tokens_grad, (gain_one_grad, qkv_grad, out_grad, gain_two_grad, in_grad, down_grad))

def reference(tokens, cotangent, attn_gain, w_qkv, w_attn_out, mlp_gain, w_in, w_mlp_out):
    sequences = tokens.reshape(N_DP, SEQ_LEN, D)
    cot_seqs = cotangent.reshape(N_DP, SEQ_LEN, D)
    zero_sums = (jnp.zeros((D,), jnp.float32), jnp.zeros((D, 3, D), jnp.float32), jnp.zeros((D, D), jnp.float32), jnp.zeros((D,), jnp.float32), jnp.zeros((D, 2, FF), jnp.float32), jnp.zeros((FF, D), jnp.float32))

    def one_step(running, pair):
        output, tokens_grad, grads = one_sequence(pair[0], pair[1], attn_gain, w_qkv, w_attn_out, mlp_gain, w_in, w_mlp_out)
        summed = tuple((left + right for left, right in zip(running, grads)))
        return (summed, (output, tokens_grad))
    sums, (outputs, input_grads) = lax.scan(one_step, zero_sums, (sequences, cot_seqs))
    return (outputs.reshape(TOKENS, D), input_grads.reshape(TOKENS, D), sums[0], sums[1], sums[2], sums[3], sums[4], sums[5])
```

```python
import functools

import jax
import jax.numpy as jnp
import numpy as np
from jax import lax
from jax.experimental import pallas as pl
from jax.experimental.pallas import tpu as pltpu
from jax.sharding import PartitionSpec as P

MESH = pl.DeviceIdType.MESH
PAIR = 2
BF = jnp.bfloat16
F32 = jnp.float32

HEAD_DIM = 64


norm_eps = 1e-05
rope_base = 160000.0
query_block = 512


def rotary_tables(length, head_width):
    half_width = head_width // 2
    freqs = rope_base ** (-(jnp.arange(half_width, dtype=jnp.float32) * 2.0 / head_width))
    angles = jnp.arange(length, dtype=jnp.float32)[:, None] * freqs[None, :]
    angles = jnp.concatenate([angles, angles], axis=1)
    return (jnp.cos(angles), jnp.sin(angles))


def rotate_half(values):
    half_width = values.shape[-1] // 2
    return jnp.concatenate([-values[..., half_width:], values[..., :half_width]], axis=-1)


def apply_rotary(values, cosine_table, sine_table):
    return values * cosine_table[:, None, :] + rotate_half(values) * sine_table[:, None, :]


def undo_rotary(grads, cosine_table, sine_table):
    return grads * cosine_table[:, None, :] - rotate_half(grads * sine_table[:, None, :])


def norm_stats(values):
    centered = values - jnp.mean(values, axis=-1, keepdims=True)
    variance = jnp.mean(centered * centered, axis=-1, keepdims=True)
    inverse = lax.rsqrt(variance + norm_eps)
    return (centered * inverse, inverse)


def norm_backward(grad_out, normed, inverse, gain_vals):
    scaled = grad_out * gain_vals
    grad_in = inverse * (
        scaled
        - jnp.mean(scaled, axis=-1, keepdims=True)
        - normed * jnp.mean(scaled * normed, axis=-1, keepdims=True)
    )
    return (grad_in, jnp.sum(grad_out * normed, axis=0))


def gelu_exact(values):
    return 0.5 * values * (1.0 + jax.scipy.special.erf(values * 0.7071067811865476))


def gelu_slope(values):
    return (
        0.5 * (1.0 + jax.scipy.special.erf(values * 0.7071067811865476))
        + values * jnp.exp(-0.5 * values * values) * 0.3989422804014327
    )


def contract_rows(left, right):
    return lax.dot_general(
        left, right, (((0,), (0,)), ((), ())), preferred_element_type=jnp.float32
    )


def times_transposed(left, right):
    return lax.dot_general(
        left, right, (((1,), (1,)), ((), ())), preferred_element_type=jnp.float32
    )


def attention_weights(attn_gain, w_qkv, w_attn_out):
    return (
        lax.all_gather(attn_gain, "dp", axis=0, tiled=True),
        lax.all_gather(w_qkv, "dp", axis=0, tiled=True),
        lax.all_gather(w_attn_out, "dp", axis=1, tiled=True),
    )


def feedforward_weights(mlp_gain, w_in, w_mlp_out):
    return (
        lax.all_gather(mlp_gain, "dp", axis=0, tiled=True),
        lax.all_gather(w_in, "dp", axis=0, tiled=True),
        lax.all_gather(w_mlp_out, "dp", axis=1, tiled=True),
    )


def attention_forward(queries, key_rows, value_rows):
    length, head_count, head_width = queries.shape
    block_size = min(query_block, length)
    score_scale = head_width ** (-0.5)
    blocks = queries.reshape(length // block_size, block_size, head_count, head_width)

    def one_block(block_rows):
        scores = (
            jnp.einsum("qhd,khd->hqk", block_rows, key_rows, preferred_element_type=jnp.float32)
            * score_scale
        )
        row_peak = jnp.max(scores, axis=-1, keepdims=True)
        exp_scores = jnp.exp(scores - row_peak)
        row_total = jnp.sum(exp_scores, axis=-1, keepdims=True)
        attn_probs = (exp_scores / row_total).astype(jnp.bfloat16)
        block_out = jnp.einsum(
            "hqk,khd->qhd", attn_probs, value_rows, preferred_element_type=jnp.float32
        )
        return (block_out.astype(jnp.bfloat16), (row_peak + jnp.log(row_total))[..., 0])

    outs, log_totals = lax.map(one_block, blocks)
    return (outs.reshape(length, head_count, head_width), log_totals)


def attention_backward(queries, key_rows, value_rows, attended, log_totals, grad_out):
    length, head_count, head_width = queries.shape
    block_size = min(query_block, length)
    nblocks = length // block_size
    score_scale = head_width ** (-0.5)

    def one_block(running, block_inputs):
        key_grad, value_grad = running
        block_rows, out_rows, grad_rows, lse_rows = block_inputs
        scores = (
            jnp.einsum("qhd,khd->hqk", block_rows, key_rows, preferred_element_type=jnp.float32)
            * score_scale
        )
        attn_probs = jnp.exp(scores - lse_rows[..., None])
        value_grad = value_grad + jnp.einsum(
            "hqk,qhd->khd",
            attn_probs.astype(jnp.bfloat16),
            grad_rows,
            preferred_element_type=jnp.float32,
        )
        dprobs = jnp.einsum(
            "qhd,khd->hqk", grad_rows, value_rows, preferred_element_type=jnp.float32
        )
        row_delta = jnp.sum(grad_rows.astype(jnp.float32) * out_rows.astype(jnp.float32), axis=-1).T
        dscores = (attn_probs * (dprobs - row_delta[..., None]) * score_scale).astype(jnp.bfloat16)
        query_grad = jnp.einsum(
            "hqk,khd->qhd", dscores, key_rows, preferred_element_type=jnp.float32
        )
        key_grad = key_grad + jnp.einsum(
            "hqk,qhd->khd", dscores, block_rows, preferred_element_type=jnp.float32
        )
        return ((key_grad, value_grad), query_grad)

    zero_grad = jnp.zeros((length, head_count, head_width), jnp.float32)
    shape_blocks = (nblocks, block_size, head_count, head_width)
    block_inputs = (
        queries.reshape(shape_blocks),
        attended.reshape(shape_blocks),
        grad_out.reshape(shape_blocks),
        log_totals,
    )
    (key_grad, value_grad), query_grad = lax.scan(one_block, (zero_grad, zero_grad), block_inputs)
    return (query_grad.reshape(length, head_count, head_width), key_grad, value_grad)


def shards(tokens, cotangent, attn_gain, w_qkv, w_attn_out, mlp_gain, w_in, w_mlp_out):
    gain_one, qkv_full, out_full = attention_weights(attn_gain, w_qkv, w_attn_out)
    gain_two, in_full, down_full = feedforward_weights(mlp_gain, w_in, w_mlp_out)
    model_width = tokens.shape[1]
    residual = tokens.astype(jnp.float32)
    normed_one, inverse_one = norm_stats(residual)
    first_in = (normed_one * gain_one.astype(jnp.float32)).astype(jnp.bfloat16)
    first_all = lax.all_gather(first_in, "mp", axis=0, tiled=True)
    length = first_all.shape[0]
    local_width = qkv_full.shape[2]
    head_count = local_width // HEAD_DIM
    cosine_table, sine_table = rotary_tables(length, HEAD_DIM)
    projected = jnp.dot(
        first_all,
        qkv_full.reshape(model_width, 3 * local_width),
        preferred_element_type=jnp.float32,
    )
    projected = projected.reshape(length, 3, head_count, HEAD_DIM)
    queries = apply_rotary(projected[:, 0], cosine_table, sine_table).astype(jnp.bfloat16)
    key_rows = apply_rotary(projected[:, 1], cosine_table, sine_table).astype(jnp.bfloat16)
    value_rows = projected[:, 2].astype(jnp.bfloat16)
    attended, log_totals = attention_forward(queries, key_rows, value_rows)
    attended_flat = attended.reshape(length, local_width)
    mixed_rows = residual + lax.psum_scatter(
        jnp.dot(attended_flat, out_full, preferred_element_type=jnp.float32),
        "mp",
        scatter_dimension=0,
        tiled=True,
    )
    normed_two, inverse_two = norm_stats(mixed_rows)
    second_in = (normed_two * gain_two.astype(jnp.float32)).astype(jnp.bfloat16)
    second_all = lax.all_gather(second_in, "mp", axis=0, tiled=True)
    unit_count = in_full.shape[2]
    lifted = jnp.dot(
        second_all, in_full.reshape(model_width, 2 * unit_count), preferred_element_type=jnp.float32
    )
    lifted = lifted.reshape(length, 2, unit_count)
    inputs = lifted[:, 0]
    gate_vals = lifted[:, 1]
    activated = gelu_exact(inputs)
    hidden = (activated * gate_vals).astype(jnp.bfloat16)
    output = mixed_rows + lax.psum_scatter(
        jnp.dot(hidden, down_full, preferred_element_type=jnp.float32).astype(jnp.bfloat16),
        "mp",
        scatter_dimension=0,
        tiled=True,
    ).astype(jnp.float32)
    gain_two, in_full, down_full = feedforward_weights(mlp_gain, w_in, w_mlp_out)
    gain_one, qkv_full, out_full = attention_weights(attn_gain, w_qkv, w_attn_out)
    cot_all = lax.all_gather(cotangent, "mp", axis=0, tiled=True)
    hidden_grad = times_transposed(cot_all, down_full)
    down_grad = contract_rows(hidden, cot_all)
    input_grad = hidden_grad * gate_vals * gelu_slope(inputs)
    gate_grad = hidden_grad * activated
    lifted_grad = (
        jnp.stack([input_grad, gate_grad], axis=1)
        .astype(jnp.bfloat16)
        .reshape(length, 2 * unit_count)
    )
    in_grad = contract_rows(second_all, lifted_grad).reshape(model_width, 2, unit_count)
    in_flat = in_full.reshape(model_width, 2 * unit_count)
    second_grad = lax.psum_scatter(
        times_transposed(lifted_grad, in_flat), "mp", scatter_dimension=0, tiled=True
    )
    back_two, gain_two_part = norm_backward(
        second_grad, normed_two, inverse_two, gain_two.astype(jnp.float32)
    )
    mixed_grad = cotangent.astype(jnp.float32) + back_two
    mixed_low = mixed_grad.astype(jnp.bfloat16)
    mixed_all = lax.all_gather(mixed_low, "mp", axis=0, tiled=True)
    attended_grad = (
        times_transposed(mixed_all, out_full)
        .astype(jnp.bfloat16)
        .reshape(length, head_count, HEAD_DIM)
    )
    out_grad = contract_rows(attended_flat, mixed_all)
    query_grad, key_grad, value_grad = attention_backward(
        queries, key_rows, value_rows, attended, log_totals, attended_grad
    )
    query_grad = undo_rotary(query_grad, cosine_table, sine_table)
    key_grad = undo_rotary(key_grad, cosine_table, sine_table)
    projected_grad = (
        jnp.stack([query_grad, key_grad, value_grad], axis=1)
        .astype(jnp.bfloat16)
        .reshape(length, 3 * local_width)
    )
    qkv_grad = contract_rows(first_all, projected_grad).reshape(model_width, 3, local_width)
    qkv_flat = qkv_full.reshape(model_width, 3 * local_width)
    first_grad = lax.psum_scatter(
        times_transposed(projected_grad, qkv_flat).astype(jnp.bfloat16),
        "mp",
        scatter_dimension=0,
        tiled=True,
    ).astype(jnp.float32)
    back_one, gain_one_part = norm_backward(
        first_grad, normed_one, inverse_one, gain_one.astype(jnp.float32)
    )
    tokens_grad = mixed_grad + back_one
    down_shard, in_shard, gain_two_shard, out_shard, qkv_shard, gain_one_shard = (
        lax.psum_scatter(down_grad, "dp", scatter_dimension=1, tiled=True),
        lax.psum_scatter(in_grad, "dp", scatter_dimension=0, tiled=True),
        lax.psum_scatter(gain_two_part, "dp", scatter_dimension=0, tiled=True),
        lax.psum_scatter(out_grad, "dp", scatter_dimension=1, tiled=True),
        lax.psum_scatter(qkv_grad, "dp", scatter_dimension=0, tiled=True),
        lax.psum_scatter(gain_one_part, "dp", scatter_dimension=0, tiled=True),
    )
    gain_one_grad, gain_two_grad = lax.psum((gain_one_shard, gain_two_shard), "mp")
    return (
        output,
        tokens_grad,
        gain_one_grad,
        qkv_shard,
        out_shard,
        gain_two_grad,
        in_shard,
        down_shard,
    )


def nn(left, right):
    return lax.dot_general(left, right, (((1,), (0,)), ((), ())), preferred_element_type=F32)


def nt(left, right):
    return lax.dot_general(left, right, (((1,), (1,)), ((), ())), preferred_element_type=F32)


def tn(left, right):
    return lax.dot_general(left, right, (((0,), (0,)), ((), ())), preferred_element_type=F32)


def erf(x):
    return lax.erf(x)


def swap_halves(tile):
    lane = lax.broadcasted_iota(jnp.int32, tile.shape, 1)
    half = HEAD_DIM // 2
    back = pltpu.roll(tile, tile.shape[1] - half, 1)
    ahead = pltpu.roll(tile, half, 1)
    return jnp.where(lax.rem(lane, HEAD_DIM) < half, back, ahead)


def layer_kernel(
    ndp, heads,
    tok, cot, gpad, gcol, wq, wo, wi, wd, cos_t, sin_t,
    out_o, tg_o, gg_o, dq_o, do_o, di_o, dd_o,
    gains, wqf, wof, wif, wdf,
    x1, x2, xc, x3, xt1, xt2, xtc, xt3,
    qk, vb, att, pbuf, hid, actb, gateb, slopeb, lg, pg, gatt, dqs, dks, dvs,
    xh1, xh2, mixed, mgrad,
    rs_sc, rs_rc, rs_sy, rs_ry, rs_own,
    gsq, grq, gzq, gyq, gwq,
    gso, gro, gzo, gyo, gwo,
    gsi, gri, gzi, gyi, gwi,
    gsd, grd, gzd, gyd, gwd,
    ggs, ggr,
    send_sem, recv_sem,
):
    rows, width = tok.shape
    nmp = x1.shape[0]
    length = nmp * rows
    na = ndp // PAIR
    dp = lax.axis_index("dp")
    mp = lax.axis_index("mp")
    za = dp // PAIR
    zb = lax.rem(dp, PAIR)
    core = lax.rem(mp, 2)
    ypos = mp // 2
    mate = mp + 1 - 2 * core
    ypeer = mp + 2 - 4 * ypos
    diag = mate + 2 - 4 * ypos
    xpeer = za * PAIR + (1 - zb)
    local_width = heads * HEAD_DIM
    units = hid.shape[1]
    shard = wq.shape[0]

    def at_dp(d):
        return {"dp": d, "mp": mp}

    def at_mp(m):
        return {"dp": dp, "mp": m}

    counter = [0]
    sends = []

    def slot():
        counter[0] += 1
        return counter[0] - 1

    def put(src, dst, sem, dev):
        copy = pltpu.make_async_remote_copy(
            src_ref=src, dst_ref=dst, send_sem=send_sem.at[sem], recv_sem=recv_sem.at[sem],
            device_id=dev, device_id_type=MESH,
        )
        copy.start()
        sends.append(copy)

    def got(buf, sem):
        pltpu.make_async_remote_copy(
            src_ref=buf, dst_ref=buf, send_sem=send_sem.at[sem], recv_sem=recv_sem.at[sem],
            device_id=at_mp(mate), device_id_type=MESH,
        ).wait_recv()

    barrier = pltpu.get_barrier_semaphore()
    for k in range(1, ndp):
        pl.semaphore_signal(barrier, inc=1, device_id=at_dp(lax.rem(dp + k, ndp)), device_id_type=MESH)
    for other in (mate, ypeer, diag):
        pl.semaphore_signal(barrier, inc=1, device_id=at_mp(other), device_id_type=MESH)
    pl.semaphore_wait(barrier, ndp - 1 + 3)

    gain_slots = [slot() for _ in range(ndp - 1)]
    for k in range(1, ndp):
        put(gpad, gains.at[dp], gain_slots[k - 1], at_dp(lax.rem(dp + k, ndp)))

    def gather_start(src, full):
        zs = [slot() for _ in range(na)]
        xs = [slot() for _ in range(na)]
        for k in range(1, na):
            put(src, full.at[dp], zs[k], at_dp(lax.rem(za + k, na) * PAIR + zb))
        put(src, full.at[dp], xs[0], at_dp(xpeer))
        full[dp] = src[...]
        return (full, zs, xs)

    def gather_forward(state):
        full, zs, xs = state
        for k in range(1, na):
            source = lax.rem(za + na - k, na) * PAIR + zb
            got(full.at[source], zs[k])
            put(full.at[source], full.at[source], xs[k], at_dp(xpeer))

    def gather_end(state):
        full, zs, xs = state
        for k in range(na):
            source = lax.rem(za + na - k, na) * PAIR + (1 - zb)
            got(full.at[source], xs[k])

    def spread_start(buf):
        sems = [slot() for _ in range(3)]
        put(buf.at[mp], buf.at[mp], sems[0], at_mp(ypeer))
        put(buf.at[mp], buf.at[mp], sems[1], at_mp(mate))
        return (buf, sems)

    def spread_forward(state):
        buf, sems = state
        got(buf.at[ypeer], sems[0])
        put(buf.at[ypeer], buf.at[ypeer], sems[2], at_mp(mate))
        got(buf.at[mate], sems[1])

    def spread_end(state):
        buf, sems = state
        got(buf.at[diag], sems[2])

    def scatter_sum(i, part):
        s0, s1, s2 = slot(), slot(), slot()
        far_mate = 2 * (1 - ypos) + (1 - core)
        rs_sc[i, 0] = part(far_mate).astype(BF)
        put(rs_sc.at[i, 0], rs_rc.at[i, 0], s0, at_mp(mate))
        rs_sc[i, 1] = part(mate).astype(BF)
        put(rs_sc.at[i, 1], rs_rc.at[i, 1], s1, at_mp(mate))
        far = part(ypeer)
        got(rs_rc.at[i, 0], s0)
        rs_sy[i] = (far + rs_rc[i, 0].astype(F32)).astype(BF)
        put(rs_sy.at[i], rs_ry.at[i], s2, at_mp(ypeer))
        rs_own[i] = part(mp)
        return (i, s1, s2)

    def scatter_end(state):
        i, s1, s2 = state
        got(rs_rc.at[i, 1], s1)
        near = rs_own[i] + rs_rc[i, 1].astype(F32)
        got(rs_ry.at[i], s2)
        return near + rs_ry[i].astype(F32)

    def norm(vals):
        centered = vals - jnp.mean(vals, axis=-1, keepdims=True)
        inv = lax.rsqrt(jnp.mean(centered * centered, axis=-1, keepdims=True) + norm_eps)
        return centered * inv, inv

    def norm_back(grad, normed, inv, gain):
        scaled = grad * gain
        return inv * (
            scaled
            - jnp.mean(scaled, axis=-1, keepdims=True)
            - normed * jnp.mean(scaled * normed, axis=-1, keepdims=True)
        )

    def turn(buf, dst):
        @pl.loop(0, nmp)
        def _(r):
            cols = pl.ds(pl.multiple_of(r * rows, rows), rows)
            flipped = buf[r].T
            dst[:, :, :, cols] = flipped.reshape(na, PAIR, shard, rows)

    def grad_start(xt, right, gs, gr, gw):
        sems = [slot() for _ in range(na)]
        cols = right.shape[1]
        part = nn(xt[:, 1 - zb].reshape(na * shard, length), right)
        gs[...] = part.astype(BF).reshape(na, shard, cols)
        for k in [*range(1, na), 0]:
            a = lax.rem(za + k, na)
            put(gs.at[a], gr.at[a], sems[k], at_dp(xpeer))
        gw[...] = nn(xt[:, zb].reshape(na * shard, length), right).reshape(na, shard, cols)
        return (sems, gr, gw)

    def grad_middle(state, gz, gy):
        sems, gr, gw = state
        zs = [slot() for _ in range(na)]
        for k in range(1, na):
            a = lax.rem(za + k, na)
            got(gr.at[a], sems[k])
            gz[k] = (gw[a] + gr[a].astype(F32)).astype(BF)
            put(gz.at[k], gy.at[k], zs[k], at_dp(a * PAIR + zb))
        got(gr.at[za], sems[0])
        return (zs, gr, gw, gy)

    def grad_end(state):
        zs, gr, gw, gy = state
        total = gw[za] + gr[za].astype(F32)
        for k in range(1, na):
            got(gy.at[k], zs[k])
            total = total + gy[k].astype(F32)
        return total

    def tiles(count):
        return [slice(i * 128, (i + 1) * 128) for i in range(count)]

    ag_q = gather_start(wq, wqf)
    gains[dp] = gpad[...]
    for k in range(1, ndp):
        source = lax.rem(dp + ndp - k, ndp)
        got(gains.at[source], gain_slots[k - 1])
    gain_all = gains[0]
    for k in range(1, ndp):
        gain_all = gain_all + gains[k]
    gain_one = gain_all[:, :width]
    gain_two = gain_all[:, width:]

    residual = tok[...].astype(F32)
    normed_one, inv_one = norm(residual)
    xh1[...] = normed_one
    x1[mp] = (normed_one * gain_one).astype(BF)
    sp1 = spread_start(x1)
    ag_o = gather_start(wo, wof)
    spread_forward(sp1)
    xc[mp] = cot[...]
    spc = spread_start(xc)
    gather_forward(ag_q)
    ag_i = gather_start(wi, wif)
    ag_d = gather_start(wd, wdf)
    spread_end(sp1)
    spread_forward(spc)
    spread_end(spc)
    turn(x1, xt1)
    turn(xc, xtc)
    gather_end(ag_q)

    @pl.loop(0, nmp)
    def _(r):
        at = pl.ds(pl.multiple_of(r * rows, rows), rows)
        proj = nn(x1[r], wqf[...].reshape(width, 3 * local_width))
        for t in tiles(2 * local_width // 128):
            u = proj[:, t]
            qk[at, t] = (u * cos_t[at, :] + swap_halves(u) * sin_t[at, :]).astype(BF)
        vb[at, :] = proj[:, 2 * local_width :].astype(BF)

    gather_forward(ag_o)
    scale = HEAD_DIM ** (-0.5)

    def head(ref, h, at=slice(None)):
        return ref[at, h * HEAD_DIM : (h + 1) * HEAD_DIM]

    @pl.loop(0, nmp)
    def _(r):
        at = pl.ds(pl.multiple_of(r * rows, rows), rows)
        outs = []
        for h in range(heads):
            scores = nt(head(qk, h, at), head(qk, heads + h)) * scale
            peak = jnp.max(scores, axis=-1, keepdims=True)
            e = jnp.exp(scores - peak)
            probs = e / jnp.sum(e, axis=-1, keepdims=True)
            pbuf[h, at, :] = probs
            outs.append(nn(probs.astype(BF), head(vb, h)))
        att[at, :] = jnp.concatenate(outs, axis=1).astype(BF)

    gather_end(ag_o)

    def chunk(r):
        return pl.ds(pl.multiple_of(r * rows, rows), rows)

    def attn_part(r):
        return nt(att[chunk(r), :], wof[...].reshape(width, local_width))

    rs_a = scatter_sum(0, attn_part)
    gather_forward(ag_i)
    gather_forward(ag_d)
    mixed[...] = residual + scatter_end(rs_a)
    normed_two, inv_two = norm(mixed[...])
    xh2[...] = normed_two
    x2[mp] = (normed_two * gain_two).astype(BF)
    sp2 = spread_start(x2)
    gather_end(ag_i)
    gather_end(ag_d)
    spread_forward(sp2)
    spread_end(sp2)

    @pl.loop(0, nmp)
    def _(r):
        at = chunk(r)
        lifted = nn(x2[r], wif[...].reshape(width, 2 * units))
        u = lifted[:, :units]
        gate = lifted[:, units:]
        cdf = 0.5 * (1.0 + erf(u * 0.7071067811865476))
        act = u * cdf
        slope = cdf + u * jnp.exp(-0.5 * u * u) * 0.3989422804014327
        hid[at, :] = (act * gate).astype(BF)
        hgrad = nn(xc[r], wdf[...].reshape(width, units))
        lg[at, :] = jnp.concatenate([hgrad * gate * slope, hgrad * act], axis=1).astype(BF)

    def in_part(r):
        return nt(lg[chunk(r), :], wif[...].reshape(width, 2 * units))

    def down_part(r):
        return nt(hid[chunk(r), :], wdf[...].reshape(width, units))

    rs_g = scatter_sum(1, in_part)
    g_d = grad_start(xtc, hid[...], gsd, grd, gwd)
    back_two = norm_back(scatter_end(rs_g), xh2[...], inv_two, gain_two)
    mgrad[...] = cot[...].astype(F32) + back_two
    x3[mp] = mgrad[...].astype(BF)
    sp3 = spread_start(x3)
    turn(x2, xt2)
    spread_forward(sp3)
    g_d = grad_middle(g_d, gzd, gyd)
    g_i = grad_start(xt2, lg[...], gsi, gri, gwi)
    spread_end(sp3)

    dks[...] = jnp.zeros_like(dks)
    dvs[...] = jnp.zeros_like(dvs)

    @pl.loop(0, nmp)
    def _(r):
        at = chunk(r)
        agrad = nn(x3[r], wof[...].reshape(width, local_width)).astype(BF)
        out_rows = att[at, :]
        for h in range(heads):
            g = agrad[:, h * HEAD_DIM : (h + 1) * HEAD_DIM]
            o = out_rows[:, h * HEAD_DIM : (h + 1) * HEAD_DIM]
            probs = pbuf[h, at, :]
            dvs[h] += tn(probs.astype(BF), g)
            dprobs = nt(g, head(vb, h))
            delta = jnp.sum(g.astype(F32) * o.astype(F32), axis=-1, keepdims=True)
            ds = (probs * (dprobs - delta) * scale).astype(BF)
            dqs[h, at, :] = nn(ds, head(qk, heads + h))
            dks[h] += tn(ds, head(qk, h, at))

    @pl.loop(0, nmp)
    def _(r):
        at = chunk(r)
        both = jnp.concatenate(
            [dqs[h, at, :] for h in range(heads)] + [dks[h, at, :] for h in range(heads)], axis=1
        )
        for t in tiles(2 * local_width // 128):
            u = both[:, t]
            pg[at, t] = (u * cos_t[at, :] - swap_halves(u) * sin_t[at, :]).astype(BF)
        pg[at, 2 * local_width :] = jnp.concatenate(
            [dvs[h, at, :] for h in range(heads)], axis=1
        ).astype(BF)

    g_q = grad_start(xt1, pg[...], gsq, grq, gwq)

    def qkv_part(r):
        return nt(pg[chunk(r), :], wqf[...].reshape(width, 3 * local_width))

    rs_f = scatter_sum(2, qkv_part)
    g_q = grad_middle(g_q, gzq, gyq)
    g_i = grad_middle(g_i, gzi, gyi)
    rs_o = scatter_sum(3, down_part)
    turn(x3, xt3)
    g_o = grad_start(xt3, att[...], gso, gro, gwo)
    back_one = norm_back(scatter_end(rs_f), xh1[...], inv_one, gain_one)
    tg_o[...] = mgrad[...] + back_one
    out_o[...] = mixed[...] + scatter_end(rs_o)
    g_o = grad_middle(g_o, gzo, gyo)
    dd_o[...] = grad_end(g_d)
    in_grad = grad_end(g_i)
    di_o[...] = in_grad
    qkv_grad = grad_end(g_q)
    dq_o[...] = qkv_grad
    sum_one = jnp.sum(qkv_grad * wq[...].astype(F32), axis=-1, keepdims=True)
    sum_two = jnp.sum(in_grad * wi[...].astype(F32), axis=-1, keepdims=True)
    lane = lax.broadcasted_iota(jnp.int32, gcol.shape, 1)
    ggs[...] = jnp.where(lane < 64, sum_one, sum_two) / gcol[...]
    gain_sems = [slot() for _ in range(3)]
    for k, other in enumerate((ypeer, mate, diag)):
        put(ggs, ggr.at[k], gain_sems[k], at_mp(other))
    do_o[...] = grad_end(g_o)
    total = ggs[...]
    for k in range(3):
        got(ggr.at[k], gain_sems[k])
        total = total + ggr[k]
    gg_o[...] = total
    for copy in sends:
        copy.wait_send()


def fused_shards(tokens, cotangent, attn_gain, w_qkv, w_attn_out, mlp_gain, w_in, w_mlp_out):
    ndp = lax.axis_size("dp")
    nmp = lax.axis_size("mp")
    rows, width = tokens.shape
    shard = w_qkv.shape[0]
    lw = w_qkv.shape[2]
    units = w_in.shape[2]
    heads = lw // HEAD_DIM
    length = rows * nmp
    na = ndp // PAIR
    place = lax.axis_index("dp") * shard
    pad = jnp.zeros((2, width), F32)
    pad = lax.dynamic_update_slice(
        pad, jnp.stack([attn_gain, mlp_gain]).astype(F32), (0, place)
    ).reshape(1, 2 * width)
    gcol = jnp.concatenate(
        [
            jnp.broadcast_to(attn_gain.astype(F32)[:, None], (shard, 64)),
            jnp.broadcast_to(mlp_gain.astype(F32)[:, None], (shard, 64)),
        ],
        axis=1,
    )
    half = HEAD_DIM // 2
    freqs = rope_base ** (-(np.arange(half, dtype=np.float32) * np.float32(2.0) / HEAD_DIM))
    angles = np.arange(length, dtype=np.float32)[:, None] * freqs.astype(np.float32)[None, :]
    cos_t = np.tile(np.cos(angles).astype(np.float32), (1, 128 // half))
    sin = np.sin(angles).astype(np.float32)
    sin_t = np.tile(np.concatenate([-sin, sin], axis=1), (1, 128 // HEAD_DIM))

    def buf(shape, dtype=BF):
        return pltpu.VMEM(shape, dtype)

    def grad_bufs(cols):
        return [
            buf((na, shard, cols)), buf((na, shard, cols)), buf((na, shard, cols)),
            buf((na, shard, cols)), buf((na, shard, cols), F32),
        ]

    nsem = 7 + 8 * na + 3 * 4 + 3 * 4 + 8 * na + 3 + 8
    scratch = [
        buf((ndp, 1, 2 * width), F32),
        buf((ndp, shard, 3 * lw)), buf((ndp, shard, lw)),
        buf((ndp, shard, 2 * units)), buf((ndp, shard, units)),
        *[buf((nmp, rows, width)) for _ in range(4)],
        *[buf((na, PAIR, shard, length)) for _ in range(4)],
        buf((length, 2 * lw)), buf((length, lw)), buf((length, lw)),
        buf((heads, length, length), F32), buf((length, units)),
        buf((8, 128)), buf((8, 128)), buf((8, 128)),
        buf((length, 2 * units)), buf((length, 3 * lw)), buf((8, 128)),
        *[buf((heads, length, HEAD_DIM), F32) for _ in range(3)],
        *[buf((rows, width), F32) for _ in range(4)],
        buf((4, 2, rows, width)), buf((4, 2, rows, width)),
        buf((4, rows, width)), buf((4, rows, width)), buf((4, rows, width), F32),
        *grad_bufs(3 * lw), *grad_bufs(lw), *grad_bufs(2 * units), *grad_bufs(units),
        buf((shard, 128), F32), buf((3, shard, 128), F32),
        pltpu.SemaphoreType.DMA((nsem,)), pltpu.SemaphoreType.DMA((nsem,)),
    ]
    vmem = pl.BlockSpec(memory_space=pltpu.VMEM)
    shapes = [
        (rows, width), (rows, width), (shard, 128), (shard, 3 * lw), (shard, lw),
        (shard, 2 * units), (shard, units),
    ]
    out, tg, gg, dq, do, di, dd = pl.pallas_call(
        functools.partial(layer_kernel, ndp, heads),
        out_shape=[jax.ShapeDtypeStruct(s, F32) for s in shapes],
        in_specs=[vmem] * 10,
        out_specs=[vmem] * 7,
        scratch_shapes=scratch,
        compiler_params=pltpu.CompilerParams(
            collective_id=0, has_side_effects=True, vmem_limit_bytes=60 * 1024 * 1024
        ),
    )(
        tokens, cotangent, pad.reshape(1, 2 * width), gcol,
        w_qkv.reshape(shard, 3 * lw), w_attn_out.T,
        w_in.reshape(shard, 2 * units), w_mlp_out.T,
        jnp.asarray(cos_t), jnp.asarray(sin_t),
    )
    return (
        out, tg, gg[:, 0], dq.reshape(shard, 3, lw), do.T, gg[:, 64],
        di.reshape(shard, 2, units), dd.T,
    )


def choose(tokens, cotangent, attn_gain, w_qkv, w_attn_out, mlp_gain, w_in, w_mlp_out):
    ndp = lax.axis_size("dp")
    shard = w_qkv.shape[0]
    fits = (
        lax.axis_size("mp") == 4
        and ndp % PAIR == 0
        and shard % 16 == 0
        and w_mlp_out.shape[1] == shard
        and tokens.shape[0] % 128 == 0
        and tokens.shape[0] <= 128
        and 2 * w_qkv.shape[2] % 128 == 0
    )
    form = fused_shards if fits else shards
    return form(tokens, cotangent, attn_gain, w_qkv, w_attn_out, mlp_gain, w_in, w_mlp_out)


def solution(mesh):
    in_specs = (
        P(("dp", "mp"), None),
        P(("dp", "mp"), None),
        P("dp"),
        P("dp", None, "mp"),
        P("mp", "dp"),
        P("dp"),
        P("dp", None, "mp"),
        P("mp", "dp"),
    )
    out_specs = (
        P(("dp", "mp"), None),
        P(("dp", "mp"), None),
        P("dp"),
        P("dp", None, "mp"),
        P("mp", "dp"),
        P("dp"),
        P("dp", None, "mp"),
        P("mp", "dp"),
    )
    return jax.shard_map(choose, mesh=mesh, in_specs=in_specs, out_specs=out_specs, check_vma=False)
```

```python
import functools

import jax
import jax.numpy as jnp
import numpy as np
from jax import lax
from jax.experimental import pallas as pl
from jax.experimental.pallas import tpu as pltpu
from jax.sharding import PartitionSpec as P

MESH = pl.DeviceIdType.MESH
PAIR = 2
BF = jnp.bfloat16
F32 = jnp.float32

HEAD_DIM = 64


norm_eps = 1e-05
rope_base = 160000.0
query_block = 512


def rotary_tables(length, head_width):
    half_width = head_width // 2
    freqs = rope_base ** (-(jnp.arange(half_width, dtype=jnp.float32) * 2.0 / head_width))
    angles = jnp.arange(length, dtype=jnp.float32)[:, None] * freqs[None, :]
    angles = jnp.concatenate([angles, angles], axis=1)
    return (jnp.cos(angles), jnp.sin(angles))


def rotate_half(values):
    half_width = values.shape[-1] // 2
    return jnp.concatenate([-values[..., half_width:], values[..., :half_width]], axis=-1)


def apply_rotary(values, cosine_table, sine_table):
    return values * cosine_table[:, None, :] + rotate_half(values) * sine_table[:, None, :]


def undo_rotary(grads, cosine_table, sine_table):
    return grads * cosine_table[:, None, :] - rotate_half(grads * sine_table[:, None, :])


def norm_stats(values):
    centered = values - jnp.mean(values, axis=-1, keepdims=True)
    variance = jnp.mean(centered * centered, axis=-1, keepdims=True)
    inverse = lax.rsqrt(variance + norm_eps)
    return (centered * inverse, inverse)


def norm_backward(grad_out, normed, inverse, gain_vals):
    scaled = grad_out * gain_vals
    grad_in = inverse * (
        scaled
        - jnp.mean(scaled, axis=-1, keepdims=True)
        - normed * jnp.mean(scaled * normed, axis=-1, keepdims=True)
    )
    return (grad_in, jnp.sum(grad_out * normed, axis=0))


def gelu_exact(values):
    return 0.5 * values * (1.0 + jax.scipy.special.erf(values * 0.7071067811865476))


def gelu_slope(values):
    return (
        0.5 * (1.0 + jax.scipy.special.erf(values * 0.7071067811865476))
        + values * jnp.exp(-0.5 * values * values) * 0.3989422804014327
    )


def contract_rows(left, right):
    return lax.dot_general(
        left, right, (((0,), (0,)), ((), ())), preferred_element_type=jnp.float32
    )


def times_transposed(left, right):
    return lax.dot_general(
        left, right, (((1,), (1,)), ((), ())), preferred_element_type=jnp.float32
    )


def attention_weights(attn_gain, w_qkv, w_attn_out):
    return (
        lax.all_gather(attn_gain, "dp", axis=0, tiled=True),
        lax.all_gather(w_qkv, "dp", axis=0, tiled=True),
        lax.all_gather(w_attn_out, "dp", axis=1, tiled=True),
    )


def feedforward_weights(mlp_gain, w_in, w_mlp_out):
    return (
        lax.all_gather(mlp_gain, "dp", axis=0, tiled=True),
        lax.all_gather(w_in, "dp", axis=0, tiled=True),
        lax.all_gather(w_mlp_out, "dp", axis=1, tiled=True),
    )


def attention_forward(queries, key_rows, value_rows):
    length, head_count, head_width = queries.shape
    block_size = min(query_block, length)
    score_scale = head_width ** (-0.5)
    blocks = queries.reshape(length // block_size, block_size, head_count, head_width)

    def one_block(block_rows):
        scores = (
            jnp.einsum("qhd,khd->hqk", block_rows, key_rows, preferred_element_type=jnp.float32)
            * score_scale
        )
        row_peak = jnp.max(scores, axis=-1, keepdims=True)
        exp_scores = jnp.exp(scores - row_peak)
        row_total = jnp.sum(exp_scores, axis=-1, keepdims=True)
        attn_probs = (exp_scores / row_total).astype(jnp.bfloat16)
        block_out = jnp.einsum(
            "hqk,khd->qhd", attn_probs, value_rows, preferred_element_type=jnp.float32
        )
        return (block_out.astype(jnp.bfloat16), (row_peak + jnp.log(row_total))[..., 0])

    outs, log_totals = lax.map(one_block, blocks)
    return (outs.reshape(length, head_count, head_width), log_totals)


def attention_backward(queries, key_rows, value_rows, attended, log_totals, grad_out):
    length, head_count, head_width = queries.shape
    block_size = min(query_block, length)
    nblocks = length // block_size
    score_scale = head_width ** (-0.5)

    def one_block(running, block_inputs):
        key_grad, value_grad = running
        block_rows, out_rows, grad_rows, lse_rows = block_inputs
        scores = (
            jnp.einsum("qhd,khd->hqk", block_rows, key_rows, preferred_element_type=jnp.float32)
            * score_scale
        )
        attn_probs = jnp.exp(scores - lse_rows[..., None])
        value_grad = value_grad + jnp.einsum(
            "hqk,qhd->khd",
            attn_probs.astype(jnp.bfloat16),
            grad_rows,
            preferred_element_type=jnp.float32,
        )
        dprobs = jnp.einsum(
            "qhd,khd->hqk", grad_rows, value_rows, preferred_element_type=jnp.float32
        )
        row_delta = jnp.sum(grad_rows.astype(jnp.float32) * out_rows.astype(jnp.float32), axis=-1).T
        dscores = (attn_probs * (dprobs - row_delta[..., None]) * score_scale).astype(jnp.bfloat16)
        query_grad = jnp.einsum(
            "hqk,khd->qhd", dscores, key_rows, preferred_element_type=jnp.float32
        )
        key_grad = key_grad + jnp.einsum(
            "hqk,qhd->khd", dscores, block_rows, preferred_element_type=jnp.float32
        )
        return ((key_grad, value_grad), query_grad)

    zero_grad = jnp.zeros((length, head_count, head_width), jnp.float32)
    shape_blocks = (nblocks, block_size, head_count, head_width)
    block_inputs = (
        queries.reshape(shape_blocks),
        attended.reshape(shape_blocks),
        grad_out.reshape(shape_blocks),
        log_totals,
    )
    (key_grad, value_grad), query_grad = lax.scan(one_block, (zero_grad, zero_grad), block_inputs)
    return (query_grad.reshape(length, head_count, head_width), key_grad, value_grad)


def shards(tokens, cotangent, attn_gain, w_qkv, w_attn_out, mlp_gain, w_in, w_mlp_out):
    gain_one, qkv_full, out_full = attention_weights(attn_gain, w_qkv, w_attn_out)
    gain_two, in_full, down_full = feedforward_weights(mlp_gain, w_in, w_mlp_out)
    model_width = tokens.shape[1]
    residual = tokens.astype(jnp.float32)
    normed_one, inverse_one = norm_stats(residual)
    first_in = (normed_one * gain_one.astype(jnp.float32)).astype(jnp.bfloat16)
    first_all = lax.all_gather(first_in, "mp", axis=0, tiled=True)
    length = first_all.shape[0]
    local_width = qkv_full.shape[2]
    head_count = local_width // HEAD_DIM
    cosine_table, sine_table = rotary_tables(length, HEAD_DIM)
    projected = jnp.dot(
        first_all,
        qkv_full.reshape(model_width, 3 * local_width),
        preferred_element_type=jnp.float32,
    )
    projected = projected.reshape(length, 3, head_count, HEAD_DIM)
    queries = apply_rotary(projected[:, 0], cosine_table, sine_table).astype(jnp.bfloat16)
    key_rows = apply_rotary(projected[:, 1], cosine_table, sine_table).astype(jnp.bfloat16)
    value_rows = projected[:, 2].astype(jnp.bfloat16)
    attended, log_totals = attention_forward(queries, key_rows, value_rows)
    attended_flat = attended.reshape(length, local_width)
    mixed_rows = residual + lax.psum_scatter(
        jnp.dot(attended_flat, out_full, preferred_element_type=jnp.float32),
        "mp",
        scatter_dimension=0,
        tiled=True,
    )
    normed_two, inverse_two = norm_stats(mixed_rows)
    second_in = (normed_two * gain_two.astype(jnp.float32)).astype(jnp.bfloat16)
    second_all = lax.all_gather(second_in, "mp", axis=0, tiled=True)
    unit_count = in_full.shape[2]
    lifted = jnp.dot(
        second_all, in_full.reshape(model_width, 2 * unit_count), preferred_element_type=jnp.float32
    )
    lifted = lifted.reshape(length, 2, unit_count)
    inputs = lifted[:, 0]
    gate_vals = lifted[:, 1]
    activated = gelu_exact(inputs)
    hidden = (activated * gate_vals).astype(jnp.bfloat16)
    output = mixed_rows + lax.psum_scatter(
        jnp.dot(hidden, down_full, preferred_element_type=jnp.float32).astype(jnp.bfloat16),
        "mp",
        scatter_dimension=0,
        tiled=True,
    ).astype(jnp.float32)
    gain_two, in_full, down_full = feedforward_weights(mlp_gain, w_in, w_mlp_out)
    gain_one, qkv_full, out_full = attention_weights(attn_gain, w_qkv, w_attn_out)
    cot_all = lax.all_gather(cotangent, "mp", axis=0, tiled=True)
    hidden_grad = times_transposed(cot_all, down_full)
    down_grad = contract_rows(hidden, cot_all)
    input_grad = hidden_grad * gate_vals * gelu_slope(inputs)
    gate_grad = hidden_grad * activated
    lifted_grad = (
        jnp.stack([input_grad, gate_grad], axis=1)
        .astype(jnp.bfloat16)
        .reshape(length, 2 * unit_count)
    )
    in_grad = contract_rows(second_all, lifted_grad).reshape(model_width, 2, unit_count)
    in_flat = in_full.reshape(model_width, 2 * unit_count)
    second_grad = lax.psum_scatter(
        times_transposed(lifted_grad, in_flat), "mp", scatter_dimension=0, tiled=True
    )
    back_two, gain_two_part = norm_backward(
        second_grad, normed_two, inverse_two, gain_two.astype(jnp.float32)
    )
    mixed_grad = cotangent.astype(jnp.float32) + back_two
    mixed_low = mixed_grad.astype(jnp.bfloat16)
    mixed_all = lax.all_gather(mixed_low, "mp", axis=0, tiled=True)
    attended_grad = (
        times_transposed(mixed_all, out_full)
        .astype(jnp.bfloat16)
        .reshape(length, head_count, HEAD_DIM)
    )
    out_grad = contract_rows(attended_flat, mixed_all)
    query_grad, key_grad, value_grad = attention_backward(
        queries, key_rows, value_rows, attended, log_totals, attended_grad
    )
    query_grad = undo_rotary(query_grad, cosine_table, sine_table)
    key_grad = undo_rotary(key_grad, cosine_table, sine_table)
    projected_grad = (
        jnp.stack([query_grad, key_grad, value_grad], axis=1)
        .astype(jnp.bfloat16)
        .reshape(length, 3 * local_width)
    )
    qkv_grad = contract_rows(first_all, projected_grad).reshape(model_width, 3, local_width)
    qkv_flat = qkv_full.reshape(model_width, 3 * local_width)
    first_grad = lax.psum_scatter(
        times_transposed(projected_grad, qkv_flat).astype(jnp.bfloat16),
        "mp",
        scatter_dimension=0,
        tiled=True,
    ).astype(jnp.float32)
    back_one, gain_one_part = norm_backward(
        first_grad, normed_one, inverse_one, gain_one.astype(jnp.float32)
    )
    tokens_grad = mixed_grad + back_one
    down_shard, in_shard, gain_two_shard, out_shard, qkv_shard, gain_one_shard = (
        lax.psum_scatter(down_grad, "dp", scatter_dimension=1, tiled=True),
        lax.psum_scatter(in_grad, "dp", scatter_dimension=0, tiled=True),
        lax.psum_scatter(gain_two_part, "dp", scatter_dimension=0, tiled=True),
        lax.psum_scatter(out_grad, "dp", scatter_dimension=1, tiled=True),
        lax.psum_scatter(qkv_grad, "dp", scatter_dimension=0, tiled=True),
        lax.psum_scatter(gain_one_part, "dp", scatter_dimension=0, tiled=True),
    )
    gain_one_grad, gain_two_grad = lax.psum((gain_one_shard, gain_two_shard), "mp")
    return (
        output,
        tokens_grad,
        gain_one_grad,
        qkv_shard,
        out_shard,
        gain_two_grad,
        in_shard,
        down_shard,
    )


def nn(left, right):
    return lax.dot_general(left, right, (((1,), (0,)), ((), ())), preferred_element_type=F32)


def nt(left, right):
    return lax.dot_general(left, right, (((1,), (1,)), ((), ())), preferred_element_type=F32)


def tn(left, right):
    return lax.dot_general(left, right, (((0,), (0,)), ((), ())), preferred_element_type=F32)


def erf(x):
    return lax.erf(x)


def swap_halves(tile):
    lane = lax.broadcasted_iota(jnp.int32, tile.shape, 1)
    half = HEAD_DIM // 2
    back = pltpu.roll(tile, tile.shape[1] - half, 1)
    ahead = pltpu.roll(tile, half, 1)
    return jnp.where(lax.rem(lane, HEAD_DIM) < half, back, ahead)


def layer_kernel(
    ndp, heads,
    tok, cot, gain_a, gain_b, wq_in, wo_in, wi_in, wd_in, cos_t, sin_t,
    out_o, tg_o, ga_o, gb_o, dq_o, do_o, di_o, dd_o,
    gpad, wq, wo, wi, wd,
    gains, wqf, wof, wif, wdf,
    x1, x2, xc, x3, xt1, xt2, xtc, xt3,
    qk, vb, att, pbuf, hid, actb, gateb, slopeb, lg, pg, gatt, dqs, dks, dvs,
    xh1, xh2, mixed, mgrad,
    rs_sc, rs_rc, rs_sy, rs_ry, rs_own,
    gsq, grq, gzq, gyq, gwq,
    gso, gro, gzo, gyo, gwo,
    gsi, gri, gzi, gyi, gwi,
    gsd, grd, gzd, gyd, gwd,
    ggs, ggr,
    send_sem, recv_sem,
):
    rows, width = tok.shape
    nmp = x1.shape[0]
    length = nmp * rows
    na = ndp // PAIR
    dp = lax.axis_index("dp")
    mp = lax.axis_index("mp")
    za = dp // PAIR
    zb = lax.rem(dp, PAIR)
    core = lax.rem(mp, 2)
    ypos = mp // 2
    mate = mp + 1 - 2 * core
    ypeer = mp + 2 - 4 * ypos
    diag = mate + 2 - 4 * ypos
    xpeer = za * PAIR + (1 - zb)
    local_width = heads * HEAD_DIM
    units = hid.shape[1]
    shard = wq.shape[0]

    def at_dp(d):
        return {"dp": d, "mp": mp}

    def at_mp(m):
        return {"dp": dp, "mp": m}

    counter = [0]
    sends = []

    def slot():
        counter[0] += 1
        return counter[0] - 1

    def put(src, dst, sem, dev):
        copy = pltpu.make_async_remote_copy(
            src_ref=src, dst_ref=dst, send_sem=send_sem.at[sem], recv_sem=recv_sem.at[sem],
            device_id=dev, device_id_type=MESH,
        )
        copy.start()
        sends.append(copy)

    def got(buf, sem):
        pltpu.make_async_remote_copy(
            src_ref=buf, dst_ref=buf, send_sem=send_sem.at[sem], recv_sem=recv_sem.at[sem],
            device_id=at_mp(mate), device_id_type=MESH,
        ).wait_recv()

    barrier = pltpu.get_barrier_semaphore()
    for k in range(1, ndp):
        pl.semaphore_signal(barrier, inc=1, device_id=at_dp(lax.rem(dp + k, ndp)), device_id_type=MESH)
    for other in (mate, ypeer, diag):
        pl.semaphore_signal(barrier, inc=1, device_id=at_mp(other), device_id_type=MESH)
    pl.semaphore_wait(barrier, ndp - 1 + 3)

    def place(gain):
        row = jnp.concatenate(
            [gain[...].astype(F32), jnp.zeros((1, width - shard), F32)], axis=1
        )
        return pltpu.roll(jnp.broadcast_to(row, (8, width)), dp * shard, 1)[0:1]

    gpad[:, :width] = place(gain_a)
    gpad[:, width:] = place(gain_b)
    gain_slots = [slot() for _ in range(ndp - 1)]
    for k in range(1, ndp):
        put(gpad, gains.at[dp], gain_slots[k - 1], at_dp(lax.rem(dp + k, ndp)))

    def gather_start(src, full):
        zs = [slot() for _ in range(na)]
        xs = [slot() for _ in range(na)]
        for k in range(1, na):
            put(src, full.at[dp], zs[k], at_dp(lax.rem(za + k, na) * PAIR + zb))
        put(src, full.at[dp], xs[0], at_dp(xpeer))
        full[dp] = src[...]
        return (full, zs, xs)

    def gather_forward(state):
        full, zs, xs = state
        for k in range(1, na):
            source = lax.rem(za + na - k, na) * PAIR + zb
            got(full.at[source], zs[k])
            put(full.at[source], full.at[source], xs[k], at_dp(xpeer))

    def gather_end(state):
        full, zs, xs = state
        for k in range(na):
            source = lax.rem(za + na - k, na) * PAIR + (1 - zb)
            got(full.at[source], xs[k])

    def spread_start(buf):
        sems = [slot() for _ in range(3)]
        put(buf.at[mp], buf.at[mp], sems[0], at_mp(ypeer))
        put(buf.at[mp], buf.at[mp], sems[1], at_mp(mate))
        return (buf, sems)

    def spread_forward(state):
        buf, sems = state
        got(buf.at[ypeer], sems[0])
        put(buf.at[ypeer], buf.at[ypeer], sems[2], at_mp(mate))
        got(buf.at[mate], sems[1])

    def spread_end(state):
        buf, sems = state
        got(buf.at[diag], sems[2])

    def scatter_sum(i, part):
        s0, s1, s2 = slot(), slot(), slot()
        far_mate = 2 * (1 - ypos) + (1 - core)
        rs_sc[i, 0] = part(far_mate).astype(BF)
        put(rs_sc.at[i, 0], rs_rc.at[i, 0], s0, at_mp(mate))
        rs_sc[i, 1] = part(mate).astype(BF)
        put(rs_sc.at[i, 1], rs_rc.at[i, 1], s1, at_mp(mate))
        far = part(ypeer)
        got(rs_rc.at[i, 0], s0)
        rs_sy[i] = (far + rs_rc[i, 0].astype(F32)).astype(BF)
        put(rs_sy.at[i], rs_ry.at[i], s2, at_mp(ypeer))
        rs_own[i] = part(mp)
        return (i, s1, s2)

    def scatter_end(state):
        i, s1, s2 = state
        got(rs_rc.at[i, 1], s1)
        near = rs_own[i] + rs_rc[i, 1].astype(F32)
        got(rs_ry.at[i], s2)
        return near + rs_ry[i].astype(F32)

    def norm(vals):
        centered = vals - jnp.mean(vals, axis=-1, keepdims=True)
        inv = lax.rsqrt(jnp.mean(centered * centered, axis=-1, keepdims=True) + norm_eps)
        return centered * inv, inv

    def norm_back(grad, normed, inv, gain):
        scaled = grad * gain
        return inv * (
            scaled
            - jnp.mean(scaled, axis=-1, keepdims=True)
            - normed * jnp.mean(scaled * normed, axis=-1, keepdims=True)
        )

    def flip(vals):
        high, wide = vals.shape
        more_rows, more_cols = -high % 128, -wide % 128
        if more_cols:
            vals = jnp.concatenate([vals, jnp.zeros((high, more_cols), F32)], axis=1)
        if more_rows:
            vals = jnp.concatenate([vals, jnp.zeros((more_rows, wide + more_cols), F32)], axis=0)
        return vals.T[:wide, :high]

    def column(gain):
        row = jnp.concatenate([gain[...].astype(F32), jnp.ones((1, 128 - shard), F32)], axis=1)
        return jnp.broadcast_to(row, (128, 128)).T[:shard]

    def turn(buf, dst):
        @pl.loop(0, nmp)
        def _(r):
            cols = pl.ds(pl.multiple_of(r * rows, rows), rows)
            flipped = buf[r].T
            dst[:, :, :, cols] = flipped.reshape(na, PAIR, shard, rows)

    def grad_start(xt, right, gs, gr, gw):
        sems = [slot() for _ in range(na)]
        cols = right.shape[1]
        part = nn(xt[:, 1 - zb].reshape(na * shard, length), right)
        gs[...] = part.astype(BF).reshape(na, shard, cols)
        for k in [*range(1, na), 0]:
            a = lax.rem(za + k, na)
            put(gs.at[a], gr.at[a], sems[k], at_dp(xpeer))
        return (sems, gr, gw)

    def grad_own(xt, right, gw):
        cols = right.shape[1]
        gw[...] = nn(xt[:, zb].reshape(na * shard, length), right).reshape(na, shard, cols)

    def grad_middle(state, gz, gy):
        sems, gr, gw = state
        zs = [slot() for _ in range(na)]
        for k in range(1, na):
            a = lax.rem(za + k, na)
            got(gr.at[a], sems[k])
            gz[k] = (gw[a] + gr[a].astype(F32)).astype(BF)
            put(gz.at[k], gy.at[k], zs[k], at_dp(a * PAIR + zb))
        got(gr.at[za], sems[0])
        return (zs, gr, gw, gy)

    def grad_end(state):
        zs, gr, gw, gy = state
        total = gw[za] + gr[za].astype(F32)
        for k in range(1, na):
            got(gy.at[k], zs[k])
            total = total + gy[k].astype(F32)
        return total

    def tiles(count):
        return [slice(i * 128, (i + 1) * 128) for i in range(count)]

    wq[...] = jnp.concatenate([wq_in[i] for i in range(3)], axis=1)
    ag_q = gather_start(wq, wqf)
    gains[dp] = gpad[...]
    for k in range(1, ndp):
        source = lax.rem(dp + ndp - k, ndp)
        got(gains.at[source], gain_slots[k - 1])
    gain_all = gains[0]
    for k in range(1, ndp):
        gain_all = gain_all + gains[k]
    gain_one = gain_all[:, :width]
    gain_two = gain_all[:, width:]

    residual = tok[...].astype(F32)
    normed_one, inv_one = norm(residual)
    xh1[...] = normed_one
    x1[mp] = (normed_one * gain_one).astype(BF)
    sp1 = spread_start(x1)
    wo[...] = flip(wo_in[...].astype(F32)).astype(BF)
    ag_o = gather_start(wo, wof)
    wi[...] = jnp.concatenate([wi_in[:, i, :] for i in range(2)], axis=1)
    wd[...] = flip(wd_in[...].astype(F32)).astype(BF)
    spread_forward(sp1)
    xc[mp] = cot[...]
    spc = spread_start(xc)
    gather_forward(ag_q)
    ag_i = gather_start(wi, wif)
    ag_d = gather_start(wd, wdf)
    spread_end(sp1)
    spread_forward(spc)
    spread_end(spc)
    turn(x1, xt1)
    turn(xc, xtc)
    gather_end(ag_q)

    @pl.loop(0, nmp)
    def _(r):
        at = pl.ds(pl.multiple_of(r * rows, rows), rows)
        proj = nn(x1[r], wqf[...].reshape(width, 3 * local_width))
        for t in tiles(2 * local_width // 128):
            u = proj[:, t]
            qk[at, t] = (u * cos_t[at, :] + swap_halves(u) * sin_t[at, :]).astype(BF)
        vb[at, :] = proj[:, 2 * local_width :].astype(BF)

    gather_forward(ag_o)
    scale = HEAD_DIM ** (-0.5)

    def head(ref, h, at=slice(None)):
        return ref[at, h * HEAD_DIM : (h + 1) * HEAD_DIM]

    @pl.loop(0, nmp)
    def _(r):
        at = pl.ds(pl.multiple_of(r * rows, rows), rows)
        outs = []
        for h in range(heads):
            scores = nt(head(qk, h, at), head(qk, heads + h)) * scale
            peak = jnp.max(scores, axis=-1, keepdims=True)
            e = jnp.exp(scores - peak)
            probs = e / jnp.sum(e, axis=-1, keepdims=True)
            pbuf[h, at, :] = probs
            outs.append(nn(probs.astype(BF), head(vb, h)))
        att[at, :] = jnp.concatenate(outs, axis=1).astype(BF)

    gather_end(ag_o)

    def chunk(r):
        return pl.ds(pl.multiple_of(r * rows, rows), rows)

    def attn_part(r):
        return nt(att[chunk(r), :], wof[...].reshape(width, local_width))

    rs_a = scatter_sum(0, attn_part)
    gather_forward(ag_i)
    gather_forward(ag_d)
    mixed[...] = residual + scatter_end(rs_a)
    normed_two, inv_two = norm(mixed[...])
    xh2[...] = normed_two
    x2[mp] = (normed_two * gain_two).astype(BF)
    sp2 = spread_start(x2)
    gather_end(ag_i)
    gather_end(ag_d)
    spread_forward(sp2)
    spread_end(sp2)

    @pl.loop(0, nmp)
    def _(r):
        at = chunk(r)
        lifted = nn(x2[r], wif[...].reshape(width, 2 * units))
        u = lifted[:, :units]
        gate = lifted[:, units:]
        cdf = 0.5 * (1.0 + erf(u * 0.7071067811865476))
        act = u * cdf
        slope = cdf + u * jnp.exp(-0.5 * u * u) * 0.3989422804014327
        hid[at, :] = (act * gate).astype(BF)
        hgrad = nn(xc[r], wdf[...].reshape(width, units))
        lg[at, :] = jnp.concatenate([hgrad * gate * slope, hgrad * act], axis=1).astype(BF)

    def in_part(r):
        return nt(lg[chunk(r), :], wif[...].reshape(width, 2 * units))

    def down_part(r):
        return nt(hid[chunk(r), :], wdf[...].reshape(width, units))

    rs_g = scatter_sum(1, in_part)
    g_d = grad_start(xtc, hid[...], gsd, grd, gwd)
    grad_own(xtc, hid[...], gwd)
    turn(x2, xt2)
    back_two = norm_back(scatter_end(rs_g), xh2[...], inv_two, gain_two)
    mgrad[...] = cot[...].astype(F32) + back_two
    x3[mp] = mgrad[...].astype(BF)
    sp3 = spread_start(x3)
    g_i = grad_start(xt2, lg[...], gsi, gri, gwi)
    grad_own(xt2, lg[...], gwi)
    rs_o = scatter_sum(3, down_part)
    spread_forward(sp3)
    g_d = grad_middle(g_d, gzd, gyd)
    spread_end(sp3)
    turn(x3, xt3)
    g_o = grad_start(xt3, att[...], gso, gro, gwo)

    dks[...] = jnp.zeros_like(dks)
    dvs[...] = jnp.zeros_like(dvs)

    @pl.loop(0, nmp)
    def _(r):
        at = chunk(r)
        agrad = nn(x3[r], wof[...].reshape(width, local_width)).astype(BF)
        out_rows = att[at, :]
        for h in range(heads):
            g = agrad[:, h * HEAD_DIM : (h + 1) * HEAD_DIM]
            o = out_rows[:, h * HEAD_DIM : (h + 1) * HEAD_DIM]
            probs = pbuf[h, at, :]
            dvs[h] += tn(probs.astype(BF), g)
            dprobs = nt(g, head(vb, h))
            delta = jnp.sum(g.astype(F32) * o.astype(F32), axis=-1, keepdims=True)
            ds = (probs * (dprobs - delta) * scale).astype(BF)
            dqs[h, at, :] = nn(ds, head(qk, heads + h))
            dks[h] += tn(ds, head(qk, h, at))

    g_i = grad_middle(g_i, gzi, gyi)

    @pl.loop(0, nmp)
    def _(r):
        at = chunk(r)
        both = jnp.concatenate(
            [dqs[h, at, :] for h in range(heads)] + [dks[h, at, :] for h in range(heads)], axis=1
        )
        for t in tiles(2 * local_width // 128):
            u = both[:, t]
            pg[at, t] = (u * cos_t[at, :] - swap_halves(u) * sin_t[at, :]).astype(BF)
        pg[at, 2 * local_width :] = jnp.concatenate(
            [dvs[h, at, :] for h in range(heads)], axis=1
        ).astype(BF)

    g_q = grad_start(xt1, pg[...], gsq, grq, gwq)

    def qkv_part(r):
        return nt(pg[chunk(r), :], wqf[...].reshape(width, 3 * local_width))

    rs_f = scatter_sum(2, qkv_part)
    grad_own(xt1, pg[...], gwq)
    grad_own(xt3, att[...], gwo)
    g_o = grad_middle(g_o, gzo, gyo)
    g_q = grad_middle(g_q, gzq, gyq)
    back_one = norm_back(scatter_end(rs_f), xh1[...], inv_one, gain_one)
    tg_o[...] = mgrad[...] + back_one
    out_o[...] = mixed[...] + scatter_end(rs_o)
    dd_o[...] = flip(grad_end(g_d))
    in_grad = grad_end(g_i)
    for i in range(2):
        di_o[:, i, :] = in_grad[:, i * units : (i + 1) * units]
    sum_two = jnp.sum(in_grad * wi[...].astype(F32), axis=-1, keepdims=True)
    do_o[...] = flip(grad_end(g_o))
    qkv_grad = grad_end(g_q)
    sum_one = jnp.sum(qkv_grad * wq[...].astype(F32), axis=-1, keepdims=True)
    lane = lax.broadcasted_iota(jnp.int32, (shard, 128), 1)
    sums = jnp.where(lane < 1, sum_one / column(gain_a), sum_two / column(gain_b))
    ggs[...] = flip(sums)[:8]
    gain_sems = [slot() for _ in range(3)]
    for k, other in enumerate((ypeer, mate, diag)):
        put(ggs, ggr.at[k], gain_sems[k], at_mp(other))
    for i in range(3):
        dq_o[i] = qkv_grad[:, i * local_width : (i + 1) * local_width]
    total = ggs[...]
    for k in range(3):
        got(ggr.at[k], gain_sems[k])
        total = total + ggr[k]
    ga_o[...] = total[0:1]
    gb_o[...] = total[1:2]
    for copy in sends:
        copy.wait_send()


def fused_shards(tokens, cotangent, attn_gain, w_qkv, w_attn_out, mlp_gain, w_in, w_mlp_out):
    ndp = lax.axis_size("dp")
    nmp = lax.axis_size("mp")
    rows, width = tokens.shape
    shard = w_qkv.shape[0]
    lw = w_qkv.shape[2]
    units = w_in.shape[2]
    heads = lw // HEAD_DIM
    length = rows * nmp
    na = ndp // PAIR
    half = HEAD_DIM // 2
    freqs = rope_base ** (-(np.arange(half, dtype=np.float32) * np.float32(2.0) / HEAD_DIM))
    angles = np.arange(length, dtype=np.float32)[:, None] * freqs.astype(np.float32)[None, :]
    cos_t = np.tile(np.cos(angles).astype(np.float32), (1, 128 // half))
    sin = np.sin(angles).astype(np.float32)
    sin_t = np.tile(np.concatenate([-sin, sin], axis=1), (1, 128 // HEAD_DIM))

    def buf(shape, dtype=BF):
        return pltpu.VMEM(shape, dtype)

    def grad_bufs(cols):
        return [
            buf((na, shard, cols)), buf((na, shard, cols)), buf((na, shard, cols)),
            buf((na, shard, cols)), buf((na, shard, cols), F32),
        ]

    nsem = 7 + 8 * na + 3 * 4 + 3 * 4 + 8 * na + 3 + 8
    scratch = [
        buf((1, 2 * width), F32), buf((shard, 3 * lw)), buf((shard, lw)),
        buf((shard, 2 * units)), buf((shard, units)),
        buf((ndp, 1, 2 * width), F32),
        buf((ndp, shard, 3 * lw)), buf((ndp, shard, lw)),
        buf((ndp, shard, 2 * units)), buf((ndp, shard, units)),
        *[buf((nmp, rows, width)) for _ in range(4)],
        *[buf((na, PAIR, shard, length)) for _ in range(4)],
        buf((length, 2 * lw)), buf((length, lw)), buf((length, lw)),
        buf((heads, length, length), F32), buf((length, units)),
        buf((8, 128)), buf((8, 128)), buf((8, 128)),
        buf((length, 2 * units)), buf((length, 3 * lw)), buf((8, 128)),
        *[buf((heads, length, HEAD_DIM), F32) for _ in range(3)],
        *[buf((rows, width), F32) for _ in range(4)],
        buf((4, 2, rows, width)), buf((4, 2, rows, width)),
        buf((4, rows, width)), buf((4, rows, width)), buf((4, rows, width), F32),
        *grad_bufs(3 * lw), *grad_bufs(lw), *grad_bufs(2 * units), *grad_bufs(units),
        buf((8, shard), F32), buf((3, 8, shard), F32),
        pltpu.SemaphoreType.DMA((nsem,)), pltpu.SemaphoreType.DMA((nsem,)),
    ]
    vmem = pl.BlockSpec(memory_space=pltpu.VMEM)
    shapes = [
        (rows, width), (rows, width), (1, shard), (1, shard), (3, shard, lw), (lw, shard),
        (shard, 2, units), (units, shard),
    ]
    out, tg, ga, gb, dq, do, di, dd = pl.pallas_call(
        functools.partial(layer_kernel, ndp, heads),
        out_shape=[jax.ShapeDtypeStruct(s, F32) for s in shapes],
        in_specs=[vmem] * 10,
        out_specs=[vmem] * 8,
        scratch_shapes=scratch,
        compiler_params=pltpu.CompilerParams(
            collective_id=0, has_side_effects=True, vmem_limit_bytes=60 * 1024 * 1024
        ),
    )(
        tokens, cotangent, attn_gain.reshape(1, shard), mlp_gain.reshape(1, shard),
        w_qkv.transpose(1, 0, 2), w_attn_out, w_in, w_mlp_out,
        jnp.asarray(cos_t), jnp.asarray(sin_t),
    )
    return (
        out, tg, ga.reshape(shard), dq.transpose(1, 0, 2), do, gb.reshape(shard), di, dd,
    )


def choose(tokens, cotangent, attn_gain, w_qkv, w_attn_out, mlp_gain, w_in, w_mlp_out):
    ndp = lax.axis_size("dp")
    shard = w_qkv.shape[0]
    fits = (
        lax.axis_size("mp") == 4
        and ndp % PAIR == 0
        and shard % 16 == 0
        and shard <= 128
        and w_mlp_out.shape[1] == shard
        and tokens.shape[0] % 128 == 0
        and tokens.shape[0] <= 128
        and 2 * w_qkv.shape[2] % 128 == 0
    )
    form = fused_shards if fits else shards
    return form(tokens, cotangent, attn_gain, w_qkv, w_attn_out, mlp_gain, w_in, w_mlp_out)


def solution(mesh):
    in_specs = (
        P(("dp", "mp"), None),
        P(("dp", "mp"), None),
        P("dp"),
        P("dp", None, "mp"),
        P("mp", "dp"),
        P("dp"),
        P("dp", None, "mp"),
        P("mp", "dp"),
    )
    out_specs = (
        P(("dp", "mp"), None),
        P(("dp", "mp"), None),
        P("dp"),
        P("dp", None, "mp"),
        P("mp", "dp"),
        P("dp"),
        P("dp", None, "mp"),
        P("mp", "dp"),
    )
    return jax.shard_map(choose, mesh=mesh, in_specs=in_specs, out_specs=out_specs, check_vma=False)
```

```python
import functools

import jax
import jax.numpy as jnp
import numpy as np
from jax import lax
from jax.experimental import pallas as pl
from jax.experimental.pallas import tpu as pltpu
from jax.sharding import PartitionSpec as P

MESH = pl.DeviceIdType.MESH
PAIR = 2
PARTS = 2
BF = jnp.bfloat16
F32 = jnp.float32

HEAD_DIM = 64


norm_eps = 1e-05
rope_base = 160000.0
query_block = 512


def rotary_tables(length, head_width):
    half_width = head_width // 2
    freqs = rope_base ** (-(jnp.arange(half_width, dtype=jnp.float32) * 2.0 / head_width))
    angles = jnp.arange(length, dtype=jnp.float32)[:, None] * freqs[None, :]
    angles = jnp.concatenate([angles, angles], axis=1)
    return (jnp.cos(angles), jnp.sin(angles))


def rotate_half(values):
    half_width = values.shape[-1] // 2
    return jnp.concatenate([-values[..., half_width:], values[..., :half_width]], axis=-1)


def apply_rotary(values, cosine_table, sine_table):
    return values * cosine_table[:, None, :] + rotate_half(values) * sine_table[:, None, :]


def undo_rotary(grads, cosine_table, sine_table):
    return grads * cosine_table[:, None, :] - rotate_half(grads * sine_table[:, None, :])


def norm_stats(values):
    centered = values - jnp.mean(values, axis=-1, keepdims=True)
    variance = jnp.mean(centered * centered, axis=-1, keepdims=True)
    inverse = lax.rsqrt(variance + norm_eps)
    return (centered * inverse, inverse)


def norm_backward(grad_out, normed, inverse, gain_vals):
    scaled = grad_out * gain_vals
    grad_in = inverse * (
        scaled
        - jnp.mean(scaled, axis=-1, keepdims=True)
        - normed * jnp.mean(scaled * normed, axis=-1, keepdims=True)
    )
    return (grad_in, jnp.sum(grad_out * normed, axis=0))


def gelu_exact(values):
    return 0.5 * values * (1.0 + jax.scipy.special.erf(values * 0.7071067811865476))


def gelu_slope(values):
    return (
        0.5 * (1.0 + jax.scipy.special.erf(values * 0.7071067811865476))
        + values * jnp.exp(-0.5 * values * values) * 0.3989422804014327
    )


def contract_rows(left, right):
    return lax.dot_general(
        left, right, (((0,), (0,)), ((), ())), preferred_element_type=jnp.float32
    )


def times_transposed(left, right):
    return lax.dot_general(
        left, right, (((1,), (1,)), ((), ())), preferred_element_type=jnp.float32
    )


def attention_weights(attn_gain, w_qkv, w_attn_out):
    return (
        lax.all_gather(attn_gain, "dp", axis=0, tiled=True),
        lax.all_gather(w_qkv, "dp", axis=0, tiled=True),
        lax.all_gather(w_attn_out, "dp", axis=1, tiled=True),
    )


def feedforward_weights(mlp_gain, w_in, w_mlp_out):
    return (
        lax.all_gather(mlp_gain, "dp", axis=0, tiled=True),
        lax.all_gather(w_in, "dp", axis=0, tiled=True),
        lax.all_gather(w_mlp_out, "dp", axis=1, tiled=True),
    )


def attention_forward(queries, key_rows, value_rows):
    length, head_count, head_width = queries.shape
    block_size = min(query_block, length)
    score_scale = head_width ** (-0.5)
    blocks = queries.reshape(length // block_size, block_size, head_count, head_width)

    def one_block(block_rows):
        scores = (
            jnp.einsum("qhd,khd->hqk", block_rows, key_rows, preferred_element_type=jnp.float32)
            * score_scale
        )
        row_peak = jnp.max(scores, axis=-1, keepdims=True)
        exp_scores = jnp.exp(scores - row_peak)
        row_total = jnp.sum(exp_scores, axis=-1, keepdims=True)
        attn_probs = (exp_scores / row_total).astype(jnp.bfloat16)
        block_out = jnp.einsum(
            "hqk,khd->qhd", attn_probs, value_rows, preferred_element_type=jnp.float32
        )
        return (block_out.astype(jnp.bfloat16), (row_peak + jnp.log(row_total))[..., 0])

    outs, log_totals = lax.map(one_block, blocks)
    return (outs.reshape(length, head_count, head_width), log_totals)


def attention_backward(queries, key_rows, value_rows, attended, log_totals, grad_out):
    length, head_count, head_width = queries.shape
    block_size = min(query_block, length)
    nblocks = length // block_size
    score_scale = head_width ** (-0.5)

    def one_block(running, block_inputs):
        key_grad, value_grad = running
        block_rows, out_rows, grad_rows, lse_rows = block_inputs
        scores = (
            jnp.einsum("qhd,khd->hqk", block_rows, key_rows, preferred_element_type=jnp.float32)
            * score_scale
        )
        attn_probs = jnp.exp(scores - lse_rows[..., None])
        value_grad = value_grad + jnp.einsum(
            "hqk,qhd->khd",
            attn_probs.astype(jnp.bfloat16),
            grad_rows,
            preferred_element_type=jnp.float32,
        )
        dprobs = jnp.einsum(
            "qhd,khd->hqk", grad_rows, value_rows, preferred_element_type=jnp.float32
        )
        row_delta = jnp.sum(grad_rows.astype(jnp.float32) * out_rows.astype(jnp.float32), axis=-1).T
        dscores = (attn_probs * (dprobs - row_delta[..., None]) * score_scale).astype(jnp.bfloat16)
        query_grad = jnp.einsum(
            "hqk,khd->qhd", dscores, key_rows, preferred_element_type=jnp.float32
        )
        key_grad = key_grad + jnp.einsum(
            "hqk,qhd->khd", dscores, block_rows, preferred_element_type=jnp.float32
        )
        return ((key_grad, value_grad), query_grad)

    zero_grad = jnp.zeros((length, head_count, head_width), jnp.float32)
    shape_blocks = (nblocks, block_size, head_count, head_width)
    block_inputs = (
        queries.reshape(shape_blocks),
        attended.reshape(shape_blocks),
        grad_out.reshape(shape_blocks),
        log_totals,
    )
    (key_grad, value_grad), query_grad = lax.scan(one_block, (zero_grad, zero_grad), block_inputs)
    return (query_grad.reshape(length, head_count, head_width), key_grad, value_grad)


def shards(tokens, cotangent, attn_gain, w_qkv, w_attn_out, mlp_gain, w_in, w_mlp_out):
    gain_one, qkv_full, out_full = attention_weights(attn_gain, w_qkv, w_attn_out)
    gain_two, in_full, down_full = feedforward_weights(mlp_gain, w_in, w_mlp_out)
    model_width = tokens.shape[1]
    residual = tokens.astype(jnp.float32)
    normed_one, inverse_one = norm_stats(residual)
    first_in = (normed_one * gain_one.astype(jnp.float32)).astype(jnp.bfloat16)
    first_all = lax.all_gather(first_in, "mp", axis=0, tiled=True)
    length = first_all.shape[0]
    local_width = qkv_full.shape[2]
    head_count = local_width // HEAD_DIM
    cosine_table, sine_table = rotary_tables(length, HEAD_DIM)
    projected = jnp.dot(
        first_all,
        qkv_full.reshape(model_width, 3 * local_width),
        preferred_element_type=jnp.float32,
    )
    projected = projected.reshape(length, 3, head_count, HEAD_DIM)
    queries = apply_rotary(projected[:, 0], cosine_table, sine_table).astype(jnp.bfloat16)
    key_rows = apply_rotary(projected[:, 1], cosine_table, sine_table).astype(jnp.bfloat16)
    value_rows = projected[:, 2].astype(jnp.bfloat16)
    attended, log_totals = attention_forward(queries, key_rows, value_rows)
    attended_flat = attended.reshape(length, local_width)
    mixed_rows = residual + lax.psum_scatter(
        jnp.dot(attended_flat, out_full, preferred_element_type=jnp.float32),
        "mp",
        scatter_dimension=0,
        tiled=True,
    )
    normed_two, inverse_two = norm_stats(mixed_rows)
    second_in = (normed_two * gain_two.astype(jnp.float32)).astype(jnp.bfloat16)
    second_all = lax.all_gather(second_in, "mp", axis=0, tiled=True)
    unit_count = in_full.shape[2]
    lifted = jnp.dot(
        second_all, in_full.reshape(model_width, 2 * unit_count), preferred_element_type=jnp.float32
    )
    lifted = lifted.reshape(length, 2, unit_count)
    inputs = lifted[:, 0]
    gate_vals = lifted[:, 1]
    activated = gelu_exact(inputs)
    hidden = (activated * gate_vals).astype(jnp.bfloat16)
    output = mixed_rows + lax.psum_scatter(
        jnp.dot(hidden, down_full, preferred_element_type=jnp.float32).astype(jnp.bfloat16),
        "mp",
        scatter_dimension=0,
        tiled=True,
    ).astype(jnp.float32)
    gain_two, in_full, down_full = feedforward_weights(mlp_gain, w_in, w_mlp_out)
    gain_one, qkv_full, out_full = attention_weights(attn_gain, w_qkv, w_attn_out)
    cot_all = lax.all_gather(cotangent, "mp", axis=0, tiled=True)
    hidden_grad = times_transposed(cot_all, down_full)
    down_grad = contract_rows(hidden, cot_all)
    input_grad = hidden_grad * gate_vals * gelu_slope(inputs)
    gate_grad = hidden_grad * activated
    lifted_grad = (
        jnp.stack([input_grad, gate_grad], axis=1)
        .astype(jnp.bfloat16)
        .reshape(length, 2 * unit_count)
    )
    in_grad = contract_rows(second_all, lifted_grad).reshape(model_width, 2, unit_count)
    in_flat = in_full.reshape(model_width, 2 * unit_count)
    second_grad = lax.psum_scatter(
        times_transposed(lifted_grad, in_flat), "mp", scatter_dimension=0, tiled=True
    )
    back_two, gain_two_part = norm_backward(
        second_grad, normed_two, inverse_two, gain_two.astype(jnp.float32)
    )
    mixed_grad = cotangent.astype(jnp.float32) + back_two
    mixed_low = mixed_grad.astype(jnp.bfloat16)
    mixed_all = lax.all_gather(mixed_low, "mp", axis=0, tiled=True)
    attended_grad = (
        times_transposed(mixed_all, out_full)
        .astype(jnp.bfloat16)
        .reshape(length, head_count, HEAD_DIM)
    )
    out_grad = contract_rows(attended_flat, mixed_all)
    query_grad, key_grad, value_grad = attention_backward(
        queries, key_rows, value_rows, attended, log_totals, attended_grad
    )
    query_grad = undo_rotary(query_grad, cosine_table, sine_table)
    key_grad = undo_rotary(key_grad, cosine_table, sine_table)
    projected_grad = (
        jnp.stack([query_grad, key_grad, value_grad], axis=1)
        .astype(jnp.bfloat16)
        .reshape(length, 3 * local_width)
    )
    qkv_grad = contract_rows(first_all, projected_grad).reshape(model_width, 3, local_width)
    qkv_flat = qkv_full.reshape(model_width, 3 * local_width)
    first_grad = lax.psum_scatter(
        times_transposed(projected_grad, qkv_flat).astype(jnp.bfloat16),
        "mp",
        scatter_dimension=0,
        tiled=True,
    ).astype(jnp.float32)
    back_one, gain_one_part = norm_backward(
        first_grad, normed_one, inverse_one, gain_one.astype(jnp.float32)
    )
    tokens_grad = mixed_grad + back_one
    down_shard, in_shard, gain_two_shard, out_shard, qkv_shard, gain_one_shard = (
        lax.psum_scatter(down_grad, "dp", scatter_dimension=1, tiled=True),
        lax.psum_scatter(in_grad, "dp", scatter_dimension=0, tiled=True),
        lax.psum_scatter(gain_two_part, "dp", scatter_dimension=0, tiled=True),
        lax.psum_scatter(out_grad, "dp", scatter_dimension=1, tiled=True),
        lax.psum_scatter(qkv_grad, "dp", scatter_dimension=0, tiled=True),
        lax.psum_scatter(gain_one_part, "dp", scatter_dimension=0, tiled=True),
    )
    gain_one_grad, gain_two_grad = lax.psum((gain_one_shard, gain_two_shard), "mp")
    return (
        output,
        tokens_grad,
        gain_one_grad,
        qkv_shard,
        out_shard,
        gain_two_grad,
        in_shard,
        down_shard,
    )


def nn(left, right):
    return lax.dot_general(left, right, (((1,), (0,)), ((), ())), preferred_element_type=F32)


def nt(left, right):
    return lax.dot_general(left, right, (((1,), (1,)), ((), ())), preferred_element_type=F32)


def tn(left, right):
    return lax.dot_general(left, right, (((0,), (0,)), ((), ())), preferred_element_type=F32)


def erf(x):
    return lax.erf(x)


def swap_halves(tile):
    lane = lax.broadcasted_iota(jnp.int32, tile.shape, 1)
    half = HEAD_DIM // 2
    back = pltpu.roll(tile, tile.shape[1] - half, 1)
    ahead = pltpu.roll(tile, half, 1)
    return jnp.where(lax.rem(lane, HEAD_DIM) < half, back, ahead)


def layer_kernel(
    ndp, heads,
    tok, cot, gain_a, gain_b, wq_in, wo_in, wi_in, wd_in, cos_t, sin_t,
    out_o, tg_o, ga_o, gb_o, dq_o, do_o, di_o, dd_o,
    gpad, wq, wo, wi, wd,
    gains, wqf, wof, wif, wdf,
    x1, x2, xc, x3, xt1, xt2, xtc, xt3,
    qk, vb, att, pbuf, hid, wide, hgrad_buf, lg, pg, gatt, dqs, dks, dvs,
    xh1, xh2, mixed, mgrad,
    rs_sc, rs_rc, rs_sy, rs_ry, rs_own,
    gsq, grq, gzq, gyq, gwq,
    gso, gro, gzo, gyo, gwo,
    gsi, gri, gzi, gyi, gwi,
    gsd, grd, gzd, gyd, gwd,
    ggs, ggr,
    send_sem, recv_sem,
):
    rows, width = tok.shape
    nmp = x1.shape[0]
    length = nmp * rows
    na = ndp // PAIR
    dp = lax.axis_index("dp")
    mp = lax.axis_index("mp")
    za = dp // PAIR
    zb = lax.rem(dp, PAIR)
    core = lax.rem(mp, 2)
    ypos = mp // 2
    mate = mp + 1 - 2 * core
    ypeer = mp + 2 - 4 * ypos
    diag = mate + 2 - 4 * ypos
    xpeer = za * PAIR + (1 - zb)
    local_width = heads * HEAD_DIM
    units = hid.shape[1]
    shard = wq.shape[0]

    def at_dp(d):
        return {"dp": d, "mp": mp}

    def at_mp(m):
        return {"dp": dp, "mp": m}

    counter = [0]
    sends = []

    def slot():
        counter[0] += 1
        return counter[0] - 1

    def put(src, dst, sem, dev):
        copy = pltpu.make_async_remote_copy(
            src_ref=src, dst_ref=dst, send_sem=send_sem.at[sem], recv_sem=recv_sem.at[sem],
            device_id=dev, device_id_type=MESH,
        )
        copy.start()
        sends.append(copy)

    def got(buf, sem):
        pltpu.make_async_remote_copy(
            src_ref=buf, dst_ref=buf, send_sem=send_sem.at[sem], recv_sem=recv_sem.at[sem],
            device_id=at_mp(mate), device_id_type=MESH,
        ).wait_recv()

    barrier = pltpu.get_barrier_semaphore()
    for k in range(1, ndp):
        pl.semaphore_signal(barrier, inc=1, device_id=at_dp(lax.rem(dp + k, ndp)), device_id_type=MESH)
    for other in (mate, ypeer, diag):
        pl.semaphore_signal(barrier, inc=1, device_id=at_mp(other), device_id_type=MESH)
    pl.semaphore_wait(barrier, ndp - 1 + 3)

    def place(gain):
        row = jnp.concatenate(
            [gain[...].astype(F32), jnp.zeros((1, width - shard), F32)], axis=1
        )
        return pltpu.roll(jnp.broadcast_to(row, (8, width)), dp * shard, 1)[0:1]

    gpad[:, :width] = place(gain_a)
    gpad[:, width:] = place(gain_b)
    gain_slots = [slot() for _ in range(ndp - 1)]
    for k in range(1, ndp):
        put(gpad, gains.at[dp], gain_slots[k - 1], at_dp(lax.rem(dp + k, ndp)))

    def gather_start(src, full):
        zs = [slot() for _ in range(na)]
        xs = [slot() for _ in range(na)]
        for k in range(1, na):
            put(src, full.at[dp], zs[k], at_dp(lax.rem(za + k, na) * PAIR + zb))
        put(src, full.at[dp], xs[0], at_dp(xpeer))
        full[dp] = src[...]
        return (full, zs, xs)

    def gather_forward(state):
        full, zs, xs = state
        for k in range(1, na):
            source = lax.rem(za + na - k, na) * PAIR + zb
            got(full.at[source], zs[k])
            put(full.at[source], full.at[source], xs[k], at_dp(xpeer))

    def gather_end(state):
        full, zs, xs = state
        for k in range(na):
            source = lax.rem(za + na - k, na) * PAIR + (1 - zb)
            got(full.at[source], xs[k])

    part_rows = rows // PARTS

    def part_at(p):
        return pl.ds(p * part_rows, part_rows)

    def spread_open(buf):
        return (buf, [[slot() for _ in range(3)] for _ in range(PARTS)])

    def spread_start(state, p):
        buf, sems = state
        block = buf.at[mp, part_at(p)]
        put(block, block, sems[p][0], at_mp(ypeer))
        put(block, block, sems[p][1], at_mp(mate))

    def spread_forward(state):
        buf, sems = state
        for p in range(PARTS):
            block = buf.at[ypeer, part_at(p)]
            got(block, sems[p][0])
            put(block, block, sems[p][2], at_mp(mate))

    def spread_end(state):
        buf, sems = state
        for p in range(PARTS):
            got(buf.at[mate, part_at(p)], sems[p][1])
            got(buf.at[diag, part_at(p)], sems[p][2])

    def core_rows(ref, c):
        return jnp.concatenate([ref[chunk(c), :], ref[chunk(2 + c), :]], axis=0)

    def scatter_sum(i, left, weights):
        s_far = [slot() for _ in range(PARTS)]
        s_near = slot()
        s_y = [slot() for _ in range(PARTS)]
        other = nt(core_rows(left, 1 - core), weights)
        rs_sc[i] = other.astype(BF).reshape(2, rows, width)
        for p in range(PARTS):
            at = part_at(p)
            put(rs_sc.at[i, 1 - ypos, at], rs_rc.at[i, 1 - ypos, at], s_far[p], at_mp(mate))
        put(rs_sc.at[i, ypos], rs_rc.at[i, ypos], s_near, at_mp(mate))
        rs_own[i] = nt(core_rows(left, core), weights).reshape(2, rows, width)
        for p in range(PARTS):
            at = part_at(p)
            got(rs_rc.at[i, 1 - ypos, at], s_far[p])
            rs_sy[i, at, :] = (
                rs_own[i, 1 - ypos, at, :] + rs_rc[i, 1 - ypos, at, :].astype(F32)
            ).astype(BF)
            put(rs_sy.at[i, at], rs_ry.at[i, at], s_y[p], at_mp(ypeer))
        return (i, s_near, s_y)

    def scatter_end(state, p):
        i, s_near, s_y = state
        at = part_at(p)
        if p == 0:
            got(rs_rc.at[i, ypos], s_near)
        near = rs_own[i, ypos, at, :] + rs_rc[i, ypos, at, :].astype(F32)
        got(rs_ry.at[i, at], s_y[p])
        return near + rs_ry[i, at, :].astype(F32)

    def chunk(r):
        return pl.ds(pl.multiple_of(r * rows, rows), rows)

    def norm(vals):
        centered = vals - jnp.mean(vals, axis=-1, keepdims=True)
        inv = lax.rsqrt(jnp.mean(centered * centered, axis=-1, keepdims=True) + norm_eps)
        return centered * inv, inv

    def norm_back(grad, normed, inv, gain):
        scaled = grad * gain
        return inv * (
            scaled
            - jnp.mean(scaled, axis=-1, keepdims=True)
            - normed * jnp.mean(scaled * normed, axis=-1, keepdims=True)
        )

    def flip(vals):
        high, wide = vals.shape
        more_rows, more_cols = -high % 128, -wide % 128
        if more_cols:
            vals = jnp.concatenate([vals, jnp.zeros((high, more_cols), F32)], axis=1)
        if more_rows:
            vals = jnp.concatenate([vals, jnp.zeros((more_rows, wide + more_cols), F32)], axis=0)
        return vals.T[:wide, :high]

    def column(gain):
        row = jnp.concatenate([gain[...].astype(F32), jnp.ones((1, 128 - shard), F32)], axis=1)
        return jnp.broadcast_to(row, (128, 128)).T[:shard]

    def turn(buf, dst):
        @pl.loop(0, nmp)
        def _(r):
            cols = pl.ds(pl.multiple_of(r * rows, rows), rows)
            flipped = buf[r].T
            dst[:, :, :, cols] = flipped.reshape(na, PAIR, shard, rows)

    def grad_start(xt, right, gs, gr, gw):
        sems = [slot() for _ in range(na)]
        cols = right.shape[1]
        part = nn(xt[:, 1 - zb].reshape(na * shard, length), right)
        gs[...] = part.astype(BF).reshape(na, shard, cols)
        for k in [*range(1, na), 0]:
            a = lax.rem(za + k, na)
            put(gs.at[a], gr.at[a], sems[k], at_dp(xpeer))
        return (sems, gr, gw)

    def grad_own(xt, right, gw):
        cols = right.shape[1]
        gw[...] = nn(xt[:, zb].reshape(na * shard, length), right).reshape(na, shard, cols)

    def grad_middle(state, gz, gy):
        sems, gr, gw = state
        zs = [slot() for _ in range(na)]
        for k in range(1, na):
            a = lax.rem(za + k, na)
            got(gr.at[a], sems[k])
            gz[k] = (gw[a] + gr[a].astype(F32)).astype(BF)
            put(gz.at[k], gy.at[k], zs[k], at_dp(a * PAIR + zb))
        got(gr.at[za], sems[0])
        return (zs, gr, gw, gy)

    def grad_end(state):
        zs, gr, gw, gy = state
        total = gw[za] + gr[za].astype(F32)
        for k in range(1, na):
            got(gy.at[k], zs[k])
            total = total + gy[k].astype(F32)
        return total

    def tiles(count):
        return [slice(i * 128, (i + 1) * 128) for i in range(count)]

    wq[...] = jnp.concatenate([wq_in[i] for i in range(3)], axis=1)
    ag_q = gather_start(wq, wqf)
    gains[dp] = gpad[...]
    for k in range(1, ndp):
        source = lax.rem(dp + ndp - k, ndp)
        got(gains.at[source], gain_slots[k - 1])
    gain_all = gains[0]
    for k in range(1, ndp):
        gain_all = gain_all + gains[k]
    gain_one = gain_all[:, :width]
    gain_two = gain_all[:, width:]

    residual = tok[...].astype(F32)
    normed_one, inv_one = norm(residual)
    xh1[...] = normed_one
    x1[mp] = (normed_one * gain_one).astype(BF)
    sp1 = spread_open(x1)
    for p in range(PARTS):
        spread_start(sp1, p)
    wo[...] = flip(wo_in[...].astype(F32)).astype(BF)
    ag_o = gather_start(wo, wof)
    wi[...] = jnp.concatenate([wi_in[:, i, :] for i in range(2)], axis=1)
    wd[...] = flip(wd_in[...].astype(F32)).astype(BF)
    spread_forward(sp1)
    xc[mp] = cot[...]
    spc = spread_open(xc)
    for p in range(PARTS):
        spread_start(spc, p)
    gather_forward(ag_q)
    ag_i = gather_start(wi, wif)
    ag_d = gather_start(wd, wdf)
    spread_end(sp1)
    spread_forward(spc)
    spread_end(spc)
    turn(x1, xt1)
    turn(xc, xtc)
    gather_end(ag_q)

    wide[:, : 3 * local_width] = nn(
        x1[...].reshape(length, width), wqf[...].reshape(width, 3 * local_width)
    )

    @pl.loop(0, nmp)
    def _(r):
        at = chunk(r)
        for t in tiles(2 * local_width // 128):
            u = wide[at, t]
            qk[at, t] = (u * cos_t[at, :] + swap_halves(u) * sin_t[at, :]).astype(BF)
        vb[at, :] = wide[at, 2 * local_width : 3 * local_width].astype(BF)

    gather_forward(ag_o)
    scale = HEAD_DIM ** (-0.5)

    def head(ref, h, at=slice(None)):
        return ref[at, h * HEAD_DIM : (h + 1) * HEAD_DIM]

    block = 2 * rows

    @pl.loop(0, length // block)
    def _(r):
        at = pl.ds(pl.multiple_of(r * block, block), block)
        outs = []
        for h in range(heads):
            scores = nt(head(qk, h, at), head(qk, heads + h)) * scale
            peak = jnp.max(scores, axis=-1, keepdims=True)
            e = jnp.exp(scores - peak)
            probs = e / jnp.sum(e, axis=-1, keepdims=True)
            pbuf[h, at, :] = probs
            outs.append(nn(probs.astype(BF), head(vb, h)))
        att[at, :] = jnp.concatenate(outs, axis=1).astype(BF)

    gather_end(ag_o)

    rs_a = scatter_sum(0, att, wof[...].reshape(width, local_width))
    gather_forward(ag_i)
    inv_two = []
    sp2 = spread_open(x2)
    for p in range(PARTS):
        at = part_at(p)
        mixed[at, :] = tok[at, :].astype(F32) + scatter_end(rs_a, p)
        normed_two, inv = norm(mixed[at, :])
        inv_two.append(inv)
        xh2[at, :] = normed_two
        x2[mp, at, :] = (normed_two * gain_two).astype(BF)
        spread_start(sp2, p)
    spread_forward(sp2)
    gather_forward(ag_d)
    gather_end(ag_i)
    gather_end(ag_d)
    hgrad_buf[...] = nn(xc[...].reshape(length, width), wdf[...].reshape(width, units))
    spread_end(sp2)
    wide[:, : 2 * units] = nn(
        x2[...].reshape(length, width), wif[...].reshape(width, 2 * units)
    )

    @pl.loop(0, nmp)
    def _(r):
        at = chunk(r)
        u = wide[at, :units]
        gate = wide[at, units : 2 * units]
        cdf = 0.5 * (1.0 + erf(u * 0.7071067811865476))
        act = u * cdf
        slope = cdf + u * jnp.exp(-0.5 * u * u) * 0.3989422804014327
        hid[at, :] = (act * gate).astype(BF)
        hgrad = hgrad_buf[at, :]
        lg[at, :] = jnp.concatenate([hgrad * gate * slope, hgrad * act], axis=1).astype(BF)

    rs_g = scatter_sum(1, lg, wif[...].reshape(width, 2 * units))
    g_d = grad_start(xtc, hid[...], gsd, grd, gwd)
    grad_own(xtc, hid[...], gwd)
    turn(x2, xt2)
    sp3 = spread_open(x3)
    for p in range(PARTS):
        at = part_at(p)
        back_two = norm_back(scatter_end(rs_g, p), xh2[at, :], inv_two[p], gain_two)
        mgrad[at, :] = cot[at, :].astype(F32) + back_two
        x3[mp, at, :] = mgrad[at, :].astype(BF)
        spread_start(sp3, p)
    g_i = grad_start(xt2, lg[...], gsi, gri, gwi)
    grad_own(xt2, lg[...], gwi)
    rs_o = scatter_sum(3, hid, wdf[...].reshape(width, units))
    spread_forward(sp3)
    g_d = grad_middle(g_d, gzd, gyd)
    spread_end(sp3)
    turn(x3, xt3)
    g_o = grad_start(xt3, att[...], gso, gro, gwo)

    dks[...] = jnp.zeros_like(dks)
    dvs[...] = jnp.zeros_like(dvs)

    gatt[...] = nn(
        x3[...].reshape(length, width), wof[...].reshape(width, local_width)
    ).astype(BF)

    @pl.loop(0, length // block)
    def _(r):
        at = pl.ds(pl.multiple_of(r * block, block), block)
        agrad = gatt[at, :]
        out_rows = att[at, :]
        for h in range(heads):
            g = agrad[:, h * HEAD_DIM : (h + 1) * HEAD_DIM]
            o = out_rows[:, h * HEAD_DIM : (h + 1) * HEAD_DIM]
            probs = pbuf[h, at, :]
            dvs[h] += tn(probs.astype(BF), g)
            dprobs = nt(g, head(vb, h))
            delta = jnp.sum(g.astype(F32) * o.astype(F32), axis=-1, keepdims=True)
            ds = (probs * (dprobs - delta) * scale).astype(BF)
            dqs[h, at, :] = nn(ds, head(qk, heads + h))
            dks[h] += tn(ds, head(qk, h, at))

    g_i = grad_middle(g_i, gzi, gyi)

    @pl.loop(0, nmp)
    def _(r):
        at = chunk(r)
        both = jnp.concatenate(
            [dqs[h, at, :] for h in range(heads)] + [dks[h, at, :] for h in range(heads)], axis=1
        )
        for t in tiles(2 * local_width // 128):
            u = both[:, t]
            pg[at, t] = (u * cos_t[at, :] - swap_halves(u) * sin_t[at, :]).astype(BF)
        pg[at, 2 * local_width :] = jnp.concatenate(
            [dvs[h, at, :] for h in range(heads)], axis=1
        ).astype(BF)

    g_q = grad_start(xt1, pg[...], gsq, grq, gwq)

    rs_f = scatter_sum(2, pg, wqf[...].reshape(width, 3 * local_width))
    grad_own(xt1, pg[...], gwq)
    grad_own(xt3, att[...], gwo)
    g_o = grad_middle(g_o, gzo, gyo)
    g_q = grad_middle(g_q, gzq, gyq)
    for p in range(PARTS):
        at = part_at(p)
        own_inv = inv_one[p * part_rows : (p + 1) * part_rows]
        back_one = norm_back(scatter_end(rs_f, p), xh1[at, :], own_inv, gain_one)
        tg_o[at, :] = mgrad[at, :] + back_one
        out_o[at, :] = mixed[at, :] + scatter_end(rs_o, p)
    dd_o[...] = flip(grad_end(g_d))
    in_grad = grad_end(g_i)
    for i in range(2):
        di_o[:, i, :] = in_grad[:, i * units : (i + 1) * units]
    sum_two = jnp.sum(in_grad * wi[...].astype(F32), axis=-1, keepdims=True)
    do_o[...] = flip(grad_end(g_o))
    qkv_grad = grad_end(g_q)
    sum_one = jnp.sum(qkv_grad * wq[...].astype(F32), axis=-1, keepdims=True)
    lane = lax.broadcasted_iota(jnp.int32, (shard, 128), 1)
    sums = jnp.where(lane < 1, sum_one / column(gain_a), sum_two / column(gain_b))
    ggs[...] = flip(sums)[:8]
    gain_sems = [slot() for _ in range(3)]
    for k, other in enumerate((ypeer, mate, diag)):
        put(ggs, ggr.at[k], gain_sems[k], at_mp(other))
    for i in range(3):
        dq_o[i] = qkv_grad[:, i * local_width : (i + 1) * local_width]
    total = ggs[...]
    for k in range(3):
        got(ggr.at[k], gain_sems[k])
        total = total + ggr[k]
    ga_o[...] = total[0:1]
    gb_o[...] = total[1:2]
    for copy in sends:
        copy.wait_send()


def settle_kernel(*refs):
    count = len(refs) // 2
    for src, dst in zip(refs[:count], refs[count:]):
        dst[...] = src[...]


def fused_shards(tokens, cotangent, attn_gain, w_qkv, w_attn_out, mlp_gain, w_in, w_mlp_out):
    ndp = lax.axis_size("dp")
    nmp = lax.axis_size("mp")
    rows, width = tokens.shape
    shard = w_qkv.shape[0]
    lw = w_qkv.shape[2]
    units = w_in.shape[2]
    heads = lw // HEAD_DIM
    length = rows * nmp
    na = ndp // PAIR
    half = HEAD_DIM // 2
    freqs = rope_base ** (-(np.arange(half, dtype=np.float32) * np.float32(2.0) / HEAD_DIM))
    angles = np.arange(length, dtype=np.float32)[:, None] * freqs.astype(np.float32)[None, :]
    cos_t = np.tile(np.cos(angles).astype(np.float32), (1, 128 // half))
    sin = np.sin(angles).astype(np.float32)
    sin_t = np.tile(np.concatenate([-sin, sin], axis=1), (1, 128 // HEAD_DIM))

    def buf(shape, dtype=BF):
        return pltpu.VMEM(shape, dtype)

    def grad_bufs(cols):
        return [
            buf((na, shard, cols)), buf((na, shard, cols)), buf((na, shard, cols)),
            buf((na, shard, cols)), buf((na, shard, cols), F32),
        ]

    nsem = ndp + 16 * na + 4 * (3 * PARTS) + 4 * (2 * PARTS + 1) + 8
    scratch = [
        buf((1, 2 * width), F32), buf((shard, 3 * lw)), buf((shard, lw)),
        buf((shard, 2 * units)), buf((shard, units)),
        buf((ndp, 1, 2 * width), F32),
        buf((ndp, shard, 3 * lw)), buf((ndp, shard, lw)),
        buf((ndp, shard, 2 * units)), buf((ndp, shard, units)),
        *[buf((nmp, rows, width)) for _ in range(4)],
        *[buf((na, PAIR, shard, length)) for _ in range(4)],
        buf((length, 2 * lw)), buf((length, lw)), buf((length, lw)),
        buf((heads, length, length), F32), buf((length, units)),
        buf((length, max(3 * lw, 2 * units)), F32), buf((length, units), F32),
        buf((length, 2 * units)), buf((length, 3 * lw)), buf((length, lw)),
        *[buf((heads, length, HEAD_DIM), F32) for _ in range(3)],
        *[buf((rows, width), F32) for _ in range(4)],
        buf((4, 2, rows, width)), buf((4, 2, rows, width)),
        buf((4, rows, width)), buf((4, rows, width)), buf((4, 2, rows, width), F32),
        *grad_bufs(3 * lw), *grad_bufs(lw), *grad_bufs(2 * units), *grad_bufs(units),
        buf((8, shard), F32), buf((3, 8, shard), F32),
        pltpu.SemaphoreType.DMA((nsem,)), pltpu.SemaphoreType.DMA((nsem,)),
    ]
    vmem = pl.BlockSpec(memory_space=pltpu.VMEM)
    shapes = [
        (rows, width), (rows, width), (1, shard), (1, shard), (3, shard, lw), (lw, shard),
        (shard, 2, units), (units, shard),
    ]
    out, tg, ga, gb, dq, do, di, dd = pl.pallas_call(
        functools.partial(layer_kernel, ndp, heads),
        out_shape=[jax.ShapeDtypeStruct(s, F32) for s in shapes],
        in_specs=[vmem] * 10,
        out_specs=[vmem] * 8,
        scratch_shapes=scratch,
        compiler_params=pltpu.CompilerParams(
            collective_id=0, has_side_effects=True, vmem_limit_bytes=60 * 1024 * 1024
        ),
    )(
        tokens, cotangent, attn_gain.reshape(1, shard), mlp_gain.reshape(1, shard),
        w_qkv.transpose(1, 0, 2), w_attn_out, w_in, w_mlp_out,
        jnp.asarray(cos_t), jnp.asarray(sin_t),
    )
    out, tg, ga, gb, dq, do, di, dd = pl.pallas_call(
        settle_kernel,
        out_shape=[jax.ShapeDtypeStruct(s, F32) for s in shapes],
        in_specs=[vmem] * 8,
        out_specs=[vmem] * 8,
    )(out, tg, ga, gb, dq, do, di, dd)
    return (
        out, tg, ga.reshape(shard), dq.transpose(1, 0, 2), do, gb.reshape(shard), di, dd,
    )


def choose(tokens, cotangent, attn_gain, w_qkv, w_attn_out, mlp_gain, w_in, w_mlp_out):
    ndp = lax.axis_size("dp")
    shard = w_qkv.shape[0]
    fits = (
        lax.axis_size("mp") == 4
        and ndp % PAIR == 0
        and shard % 16 == 0
        and shard <= 128
        and w_mlp_out.shape[1] == shard
        and tokens.shape[0] % 128 == 0
        and tokens.shape[0] <= 128
        and 2 * w_qkv.shape[2] % 128 == 0
    )
    form = fused_shards if fits else shards
    return form(tokens, cotangent, attn_gain, w_qkv, w_attn_out, mlp_gain, w_in, w_mlp_out)


def solution(mesh):
    in_specs = (
        P(("dp", "mp"), None),
        P(("dp", "mp"), None),
        P("dp"),
        P("dp", None, "mp"),
        P("mp", "dp"),
        P("dp"),
        P("dp", None, "mp"),
        P("mp", "dp"),
    )
    out_specs = (
        P(("dp", "mp"), None),
        P(("dp", "mp"), None),
        P("dp"),
        P("dp", None, "mp"),
        P("mp", "dp"),
        P("dp"),
        P("dp", None, "mp"),
        P("mp", "dp"),
    )
    return jax.shard_map(choose, mesh=mesh, in_specs=in_specs, out_specs=out_specs, check_vma=False)
```

```python
import functools

import jax
import jax.numpy as jnp
import numpy as np
from jax import lax
from jax.experimental import pallas as pl
from jax.experimental.pallas import tpu as pltpu
from jax.sharding import PartitionSpec as P

MESH = pl.DeviceIdType.MESH
PAIR = 2
PARTS = 2
BF = jnp.bfloat16
F32 = jnp.float32

HEAD_DIM = 64


norm_eps = 1e-05
rope_base = 160000.0
query_block = 512


def rotary_tables(length, head_width):
    half_width = head_width // 2
    freqs = rope_base ** (-(jnp.arange(half_width, dtype=jnp.float32) * 2.0 / head_width))
    angles = jnp.arange(length, dtype=jnp.float32)[:, None] * freqs[None, :]
    angles = jnp.concatenate([angles, angles], axis=1)
    return (jnp.cos(angles), jnp.sin(angles))


def rotate_half(values):
    half_width = values.shape[-1] // 2
    return jnp.concatenate([-values[..., half_width:], values[..., :half_width]], axis=-1)


def apply_rotary(values, cosine_table, sine_table):
    return values * cosine_table[:, None, :] + rotate_half(values) * sine_table[:, None, :]


def undo_rotary(grads, cosine_table, sine_table):
    return grads * cosine_table[:, None, :] - rotate_half(grads * sine_table[:, None, :])


def norm_stats(values):
    centered = values - jnp.mean(values, axis=-1, keepdims=True)
    variance = jnp.mean(centered * centered, axis=-1, keepdims=True)
    inverse = lax.rsqrt(variance + norm_eps)
    return (centered * inverse, inverse)


def norm_backward(grad_out, normed, inverse, gain_vals):
    scaled = grad_out * gain_vals
    grad_in = inverse * (
        scaled
        - jnp.mean(scaled, axis=-1, keepdims=True)
        - normed * jnp.mean(scaled * normed, axis=-1, keepdims=True)
    )
    return (grad_in, jnp.sum(grad_out * normed, axis=0))


def gelu_exact(values):
    return 0.5 * values * (1.0 + jax.scipy.special.erf(values * 0.7071067811865476))


def gelu_slope(values):
    return (
        0.5 * (1.0 + jax.scipy.special.erf(values * 0.7071067811865476))
        + values * jnp.exp(-0.5 * values * values) * 0.3989422804014327
    )


def contract_rows(left, right):
    return lax.dot_general(
        left, right, (((0,), (0,)), ((), ())), preferred_element_type=jnp.float32
    )


def times_transposed(left, right):
    return lax.dot_general(
        left, right, (((1,), (1,)), ((), ())), preferred_element_type=jnp.float32
    )


def attention_weights(attn_gain, w_qkv, w_attn_out):
    return (
        lax.all_gather(attn_gain, "dp", axis=0, tiled=True),
        lax.all_gather(w_qkv, "dp", axis=0, tiled=True),
        lax.all_gather(w_attn_out, "dp", axis=1, tiled=True),
    )


def feedforward_weights(mlp_gain, w_in, w_mlp_out):
    return (
        lax.all_gather(mlp_gain, "dp", axis=0, tiled=True),
        lax.all_gather(w_in, "dp", axis=0, tiled=True),
        lax.all_gather(w_mlp_out, "dp", axis=1, tiled=True),
    )


def attention_forward(queries, key_rows, value_rows):
    length, head_count, head_width = queries.shape
    block_size = min(query_block, length)
    score_scale = head_width ** (-0.5)
    blocks = queries.reshape(length // block_size, block_size, head_count, head_width)

    def one_block(block_rows):
        scores = (
            jnp.einsum("qhd,khd->hqk", block_rows, key_rows, preferred_element_type=jnp.float32)
            * score_scale
        )
        row_peak = jnp.max(scores, axis=-1, keepdims=True)
        exp_scores = jnp.exp(scores - row_peak)
        row_total = jnp.sum(exp_scores, axis=-1, keepdims=True)
        attn_probs = (exp_scores / row_total).astype(jnp.bfloat16)
        block_out = jnp.einsum(
            "hqk,khd->qhd", attn_probs, value_rows, preferred_element_type=jnp.float32
        )
        return (block_out.astype(jnp.bfloat16), (row_peak + jnp.log(row_total))[..., 0])

    outs, log_totals = lax.map(one_block, blocks)
    return (outs.reshape(length, head_count, head_width), log_totals)


def attention_backward(queries, key_rows, value_rows, attended, log_totals, grad_out):
    length, head_count, head_width = queries.shape
    block_size = min(query_block, length)
    nblocks = length // block_size
    score_scale = head_width ** (-0.5)

    def one_block(running, block_inputs):
        key_grad, value_grad = running
        block_rows, out_rows, grad_rows, lse_rows = block_inputs
        scores = (
            jnp.einsum("qhd,khd->hqk", block_rows, key_rows, preferred_element_type=jnp.float32)
            * score_scale
        )
        attn_probs = jnp.exp(scores - lse_rows[..., None])
        value_grad = value_grad + jnp.einsum(
            "hqk,qhd->khd",
            attn_probs.astype(jnp.bfloat16),
            grad_rows,
            preferred_element_type=jnp.float32,
        )
        dprobs = jnp.einsum(
            "qhd,khd->hqk", grad_rows, value_rows, preferred_element_type=jnp.float32
        )
        row_delta = jnp.sum(grad_rows.astype(jnp.float32) * out_rows.astype(jnp.float32), axis=-1).T
        dscores = (attn_probs * (dprobs - row_delta[..., None]) * score_scale).astype(jnp.bfloat16)
        query_grad = jnp.einsum(
            "hqk,khd->qhd", dscores, key_rows, preferred_element_type=jnp.float32
        )
        key_grad = key_grad + jnp.einsum(
            "hqk,qhd->khd", dscores, block_rows, preferred_element_type=jnp.float32
        )
        return ((key_grad, value_grad), query_grad)

    zero_grad = jnp.zeros((length, head_count, head_width), jnp.float32)
    shape_blocks = (nblocks, block_size, head_count, head_width)
    block_inputs = (
        queries.reshape(shape_blocks),
        attended.reshape(shape_blocks),
        grad_out.reshape(shape_blocks),
        log_totals,
    )
    (key_grad, value_grad), query_grad = lax.scan(one_block, (zero_grad, zero_grad), block_inputs)
    return (query_grad.reshape(length, head_count, head_width), key_grad, value_grad)


def shards(tokens, cotangent, attn_gain, w_qkv, w_attn_out, mlp_gain, w_in, w_mlp_out):
    gain_one, qkv_full, out_full = attention_weights(attn_gain, w_qkv, w_attn_out)
    gain_two, in_full, down_full = feedforward_weights(mlp_gain, w_in, w_mlp_out)
    model_width = tokens.shape[1]
    residual = tokens.astype(jnp.float32)
    normed_one, inverse_one = norm_stats(residual)
    first_in = (normed_one * gain_one.astype(jnp.float32)).astype(jnp.bfloat16)
    first_all = lax.all_gather(first_in, "mp", axis=0, tiled=True)
    length = first_all.shape[0]
    local_width = qkv_full.shape[2]
    head_count = local_width // HEAD_DIM
    cosine_table, sine_table = rotary_tables(length, HEAD_DIM)
    projected = jnp.dot(
        first_all,
        qkv_full.reshape(model_width, 3 * local_width),
        preferred_element_type=jnp.float32,
    )
    projected = projected.reshape(length, 3, head_count, HEAD_DIM)
    queries = apply_rotary(projected[:, 0], cosine_table, sine_table).astype(jnp.bfloat16)
    key_rows = apply_rotary(projected[:, 1], cosine_table, sine_table).astype(jnp.bfloat16)
    value_rows = projected[:, 2].astype(jnp.bfloat16)
    attended, log_totals = attention_forward(queries, key_rows, value_rows)
    attended_flat = attended.reshape(length, local_width)
    mixed_rows = residual + lax.psum_scatter(
        jnp.dot(attended_flat, out_full, preferred_element_type=jnp.float32),
        "mp",
        scatter_dimension=0,
        tiled=True,
    )
    normed_two, inverse_two = norm_stats(mixed_rows)
    second_in = (normed_two * gain_two.astype(jnp.float32)).astype(jnp.bfloat16)
    second_all = lax.all_gather(second_in, "mp", axis=0, tiled=True)
    unit_count = in_full.shape[2]
    lifted = jnp.dot(
        second_all, in_full.reshape(model_width, 2 * unit_count), preferred_element_type=jnp.float32
    )
    lifted = lifted.reshape(length, 2, unit_count)
    inputs = lifted[:, 0]
    gate_vals = lifted[:, 1]
    activated = gelu_exact(inputs)
    hidden = (activated * gate_vals).astype(jnp.bfloat16)
    output = mixed_rows + lax.psum_scatter(
        jnp.dot(hidden, down_full, preferred_element_type=jnp.float32).astype(jnp.bfloat16),
        "mp",
        scatter_dimension=0,
        tiled=True,
    ).astype(jnp.float32)
    gain_two, in_full, down_full = feedforward_weights(mlp_gain, w_in, w_mlp_out)
    gain_one, qkv_full, out_full = attention_weights(attn_gain, w_qkv, w_attn_out)
    cot_all = lax.all_gather(cotangent, "mp", axis=0, tiled=True)
    hidden_grad = times_transposed(cot_all, down_full)
    down_grad = contract_rows(hidden, cot_all)
    input_grad = hidden_grad * gate_vals * gelu_slope(inputs)
    gate_grad = hidden_grad * activated
    lifted_grad = (
        jnp.stack([input_grad, gate_grad], axis=1)
        .astype(jnp.bfloat16)
        .reshape(length, 2 * unit_count)
    )
    in_grad = contract_rows(second_all, lifted_grad).reshape(model_width, 2, unit_count)
    in_flat = in_full.reshape(model_width, 2 * unit_count)
    second_grad = lax.psum_scatter(
        times_transposed(lifted_grad, in_flat), "mp", scatter_dimension=0, tiled=True
    )
    back_two, gain_two_part = norm_backward(
        second_grad, normed_two, inverse_two, gain_two.astype(jnp.float32)
    )
    mixed_grad = cotangent.astype(jnp.float32) + back_two
    mixed_low = mixed_grad.astype(jnp.bfloat16)
    mixed_all = lax.all_gather(mixed_low, "mp", axis=0, tiled=True)
    attended_grad = (
        times_transposed(mixed_all, out_full)
        .astype(jnp.bfloat16)
        .reshape(length, head_count, HEAD_DIM)
    )
    out_grad = contract_rows(attended_flat, mixed_all)
    query_grad, key_grad, value_grad = attention_backward(
        queries, key_rows, value_rows, attended, log_totals, attended_grad
    )
    query_grad = undo_rotary(query_grad, cosine_table, sine_table)
    key_grad = undo_rotary(key_grad, cosine_table, sine_table)
    projected_grad = (
        jnp.stack([query_grad, key_grad, value_grad], axis=1)
        .astype(jnp.bfloat16)
        .reshape(length, 3 * local_width)
    )
    qkv_grad = contract_rows(first_all, projected_grad).reshape(model_width, 3, local_width)
    qkv_flat = qkv_full.reshape(model_width, 3 * local_width)
    first_grad = lax.psum_scatter(
        times_transposed(projected_grad, qkv_flat).astype(jnp.bfloat16),
        "mp",
        scatter_dimension=0,
        tiled=True,
    ).astype(jnp.float32)
    back_one, gain_one_part = norm_backward(
        first_grad, normed_one, inverse_one, gain_one.astype(jnp.float32)
    )
    tokens_grad = mixed_grad + back_one
    down_shard, in_shard, gain_two_shard, out_shard, qkv_shard, gain_one_shard = (
        lax.psum_scatter(down_grad, "dp", scatter_dimension=1, tiled=True),
        lax.psum_scatter(in_grad, "dp", scatter_dimension=0, tiled=True),
        lax.psum_scatter(gain_two_part, "dp", scatter_dimension=0, tiled=True),
        lax.psum_scatter(out_grad, "dp", scatter_dimension=1, tiled=True),
        lax.psum_scatter(qkv_grad, "dp", scatter_dimension=0, tiled=True),
        lax.psum_scatter(gain_one_part, "dp", scatter_dimension=0, tiled=True),
    )
    gain_one_grad, gain_two_grad = lax.psum((gain_one_shard, gain_two_shard), "mp")
    return (
        output,
        tokens_grad,
        gain_one_grad,
        qkv_shard,
        out_shard,
        gain_two_grad,
        in_shard,
        down_shard,
    )


def nn(left, right):
    return lax.dot_general(left, right, (((1,), (0,)), ((), ())), preferred_element_type=F32)


def nt(left, right):
    return lax.dot_general(left, right, (((1,), (1,)), ((), ())), preferred_element_type=F32)


def tn(left, right):
    return lax.dot_general(left, right, (((0,), (0,)), ((), ())), preferred_element_type=F32)


def erf(x):
    return lax.erf(x)


def swap_halves(tile):
    lane = lax.broadcasted_iota(jnp.int32, tile.shape, 1)
    half = HEAD_DIM // 2
    back = pltpu.roll(tile, tile.shape[1] - half, 1)
    ahead = pltpu.roll(tile, half, 1)
    return jnp.where(lax.rem(lane, HEAD_DIM) < half, back, ahead)


def layer_kernel(
    ndp, heads,
    tok, cot, gain_a, gain_b, wq_in, wo_in, wi_in, wd_in, cos_t, sin_t,
    out_o, tg_o, ga_o, gb_o, dq_o, do_o, di_o, dd_o,
    gpad, wq, wo, wi, wd,
    gains, wqf, wof, wif, wdf,
    x1, x2, xc, x3, xt1, xt2, xtc, xt3,
    qk, vb, att, pbuf, hid, wide, hgrad_buf, lg, pg, gatt, dqs, dks, dvs,
    xh1, xh2, mixed, mgrad,
    rs_sc, rs_rc, rs_sy, rs_ry, rs_own,
    gsq, grq, gzq, gyq, gwq,
    gso, gro, gzo, gyo, gwo,
    gsi, gri, gzi, gyi, gwi,
    gsd, grd, gzd, gyd, gwd,
    ggs, ggr,
    send_sem, recv_sem,
):
    rows, width = tok.shape
    nmp = x1.shape[0]
    length = nmp * rows
    na = ndp // PAIR
    dp = lax.axis_index("dp")
    mp = lax.axis_index("mp")
    za = dp // PAIR
    zb = lax.rem(dp, PAIR)
    core = lax.rem(mp, 2)
    ypos = mp // 2
    mate = mp + 1 - 2 * core
    ypeer = mp + 2 - 4 * ypos
    diag = mate + 2 - 4 * ypos
    xpeer = za * PAIR + (1 - zb)
    local_width = heads * HEAD_DIM
    units = hid.shape[1]
    shard = wq.shape[0]

    def at_dp(d):
        return {"dp": d, "mp": mp}

    def at_mp(m):
        return {"dp": dp, "mp": m}

    counter = [0]
    sends = []

    def slot():
        counter[0] += 1
        return counter[0] - 1

    def put(src, dst, sem, dev):
        copy = pltpu.make_async_remote_copy(
            src_ref=src, dst_ref=dst, send_sem=send_sem.at[sem], recv_sem=recv_sem.at[sem],
            device_id=dev, device_id_type=MESH,
        )
        copy.start()
        sends.append(copy)

    def got(buf, sem):
        pltpu.make_async_remote_copy(
            src_ref=buf, dst_ref=buf, send_sem=send_sem.at[sem], recv_sem=recv_sem.at[sem],
            device_id=at_mp(mate), device_id_type=MESH,
        ).wait_recv()

    barrier = pltpu.get_barrier_semaphore()
    for k in range(1, ndp):
        pl.semaphore_signal(barrier, inc=1, device_id=at_dp(lax.rem(dp + k, ndp)), device_id_type=MESH)
    for other in (mate, ypeer, diag):
        pl.semaphore_signal(barrier, inc=1, device_id=at_mp(other), device_id_type=MESH)
    pl.semaphore_wait(barrier, ndp - 1 + 3)

    def place(gain):
        row = jnp.concatenate(
            [gain[...].astype(F32), jnp.zeros((1, width - shard), F32)], axis=1
        )
        return pltpu.roll(jnp.broadcast_to(row, (8, width)), dp * shard, 1)[0:1]

    gpad[:, :width] = place(gain_a)
    gpad[:, width:] = place(gain_b)
    gain_slots = [slot() for _ in range(ndp - 1)]
    for k in range(1, ndp):
        put(gpad, gains.at[dp], gain_slots[k - 1], at_dp(lax.rem(dp + k, ndp)))

    def gather_start(src, full):
        zs = [slot() for _ in range(na)]
        xs = [slot() for _ in range(na)]
        for k in range(1, na):
            put(src, full.at[dp], zs[k], at_dp(lax.rem(za + k, na) * PAIR + zb))
        put(src, full.at[dp], xs[0], at_dp(xpeer))
        full[dp] = src[...]
        return (full, zs, xs)

    def gather_forward(state):
        full, zs, xs = state
        for k in range(1, na):
            source = lax.rem(za + na - k, na) * PAIR + zb
            got(full.at[source], zs[k])
            put(full.at[source], full.at[source], xs[k], at_dp(xpeer))

    def gather_end(state):
        full, zs, xs = state
        for k in range(na):
            source = lax.rem(za + na - k, na) * PAIR + (1 - zb)
            got(full.at[source], xs[k])

    part_rows = rows // PARTS

    def part_at(p):
        return pl.ds(p * part_rows, part_rows)

    def spread_open(buf):
        return (buf, [[slot() for _ in range(3)] for _ in range(PARTS)])

    def spread_start(state, p):
        buf, sems = state
        block = buf.at[mp, part_at(p)]
        put(block, block, sems[p][0], at_mp(ypeer))
        put(block, block, sems[p][1], at_mp(mate))

    def spread_forward(state):
        buf, sems = state
        for p in range(PARTS):
            block = buf.at[ypeer, part_at(p)]
            got(block, sems[p][0])
            put(block, block, sems[p][2], at_mp(mate))

    def spread_end(state):
        buf, sems = state
        for p in range(PARTS):
            got(buf.at[mate, part_at(p)], sems[p][1])
            got(buf.at[diag, part_at(p)], sems[p][2])

    def core_rows(ref, c):
        return jnp.concatenate([ref[chunk(c), :], ref[chunk(2 + c), :]], axis=0)

    def scatter_sum(i, left, weights):
        s_far = [slot() for _ in range(PARTS)]
        s_near = slot()
        s_y = [slot() for _ in range(PARTS)]
        other = nt(core_rows(left, 1 - core), weights)
        rs_sc[i] = other.astype(BF).reshape(2, rows, width)
        for p in range(PARTS):
            at = part_at(p)
            put(rs_sc.at[i, 1 - ypos, at], rs_rc.at[i, 1 - ypos, at], s_far[p], at_mp(mate))
        put(rs_sc.at[i, ypos], rs_rc.at[i, ypos], s_near, at_mp(mate))
        rs_own[i] = nt(core_rows(left, core), weights).reshape(2, rows, width)
        for p in range(PARTS):
            at = part_at(p)
            got(rs_rc.at[i, 1 - ypos, at], s_far[p])
            rs_sy[i, at, :] = (
                rs_own[i, 1 - ypos, at, :] + rs_rc[i, 1 - ypos, at, :].astype(F32)
            ).astype(BF)
            put(rs_sy.at[i, at], rs_ry.at[i, at], s_y[p], at_mp(ypeer))
        return (i, s_near, s_y)

    def scatter_end(state, p):
        i, s_near, s_y = state
        at = part_at(p)
        if p == 0:
            got(rs_rc.at[i, ypos], s_near)
        near = rs_own[i, ypos, at, :] + rs_rc[i, ypos, at, :].astype(F32)
        got(rs_ry.at[i, at], s_y[p])
        return near + rs_ry[i, at, :].astype(F32)

    def chunk(r):
        return pl.ds(pl.multiple_of(r * rows, rows), rows)

    def norm(vals):
        centered = vals - jnp.mean(vals, axis=-1, keepdims=True)
        inv = lax.rsqrt(jnp.mean(centered * centered, axis=-1, keepdims=True) + norm_eps)
        return centered * inv, inv

    def norm_back(grad, normed, inv, gain):
        scaled = grad * gain
        return inv * (
            scaled
            - jnp.mean(scaled, axis=-1, keepdims=True)
            - normed * jnp.mean(scaled * normed, axis=-1, keepdims=True)
        )

    def flip(vals):
        high, wide = vals.shape
        more_rows, more_cols = -high % 128, -wide % 128
        if more_cols:
            vals = jnp.concatenate([vals, jnp.zeros((high, more_cols), F32)], axis=1)
        if more_rows:
            vals = jnp.concatenate([vals, jnp.zeros((more_rows, wide + more_cols), F32)], axis=0)
        return vals.T[:wide, :high]

    def column(gain):
        row = jnp.concatenate([gain[...].astype(F32), jnp.ones((1, 128 - shard), F32)], axis=1)
        return jnp.broadcast_to(row, (128, 128)).T[:shard]

    def turn(buf, dst):
        @pl.loop(0, nmp)
        def _(r):
            cols = pl.ds(pl.multiple_of(r * rows, rows), rows)
            flipped = buf[r].T
            dst[:, :, :, cols] = flipped.reshape(na, PAIR, shard, rows)

    def grad_start(xt, right, gs, gr, gw):
        sems = [slot() for _ in range(na)]
        cols = right.shape[1]
        part = nn(xt[:, 1 - zb].reshape(na * shard, length), right)
        gs[...] = part.astype(BF).reshape(na, shard, cols)
        for k in [*range(1, na), 0]:
            a = lax.rem(za + k, na)
            put(gs.at[a], gr.at[a], sems[k], at_dp(xpeer))
        return (sems, gr, gw)

    def grad_own(xt, right, gw):
        cols = right.shape[1]
        gw[...] = nn(xt[:, zb].reshape(na * shard, length), right).reshape(na, shard, cols)

    def grad_middle(state, gz, gy):
        sems, gr, gw = state
        zs = [slot() for _ in range(na)]
        for k in range(1, na):
            a = lax.rem(za + k, na)
            got(gr.at[a], sems[k])
            gz[k] = (gw[a] + gr[a].astype(F32)).astype(BF)
            put(gz.at[k], gy.at[k], zs[k], at_dp(a * PAIR + zb))
        got(gr.at[za], sems[0])
        return (zs, gr, gw, gy)

    def grad_end(state):
        zs, gr, gw, gy = state
        total = gw[za] + gr[za].astype(F32)
        for k in range(1, na):
            got(gy.at[k], zs[k])
            total = total + gy[k].astype(F32)
        return total

    def tiles(count):
        return [slice(i * 128, (i + 1) * 128) for i in range(count)]

    wq[...] = jnp.concatenate([wq_in[i] for i in range(3)], axis=1)
    ag_q = gather_start(wq, wqf)
    gains[dp] = gpad[...]
    for k in range(1, ndp):
        source = lax.rem(dp + ndp - k, ndp)
        got(gains.at[source], gain_slots[k - 1])
    gain_all = gains[0]
    for k in range(1, ndp):
        gain_all = gain_all + gains[k]
    gain_one = gain_all[:, :width]
    gain_two = gain_all[:, width:]

    residual = tok[...].astype(F32)
    normed_one, inv_one = norm(residual)
    xh1[...] = normed_one
    x1[mp] = (normed_one * gain_one).astype(BF)
    sp1 = spread_open(x1)
    for p in range(PARTS):
        spread_start(sp1, p)
    wo[...] = flip(wo_in[...].astype(F32)).astype(BF)
    ag_o = gather_start(wo, wof)
    wi[...] = jnp.concatenate([wi_in[:, i, :] for i in range(2)], axis=1)
    wd[...] = flip(wd_in[...].astype(F32)).astype(BF)
    spread_forward(sp1)
    xc[mp] = cot[...]
    spc = spread_open(xc)
    for p in range(PARTS):
        spread_start(spc, p)
    gather_forward(ag_q)
    ag_i = gather_start(wi, wif)
    ag_d = gather_start(wd, wdf)
    spread_end(sp1)
    spread_forward(spc)
    spread_end(spc)
    turn(x1, xt1)
    turn(xc, xtc)
    gather_end(ag_q)

    wide[:, : 3 * local_width] = nn(
        x1[...].reshape(length, width), wqf[...].reshape(width, 3 * local_width)
    )

    @pl.loop(0, nmp)
    def _(r):
        at = chunk(r)
        for t in tiles(2 * local_width // 128):
            u = wide[at, t]
            qk[at, t] = (u * cos_t[at, :] + swap_halves(u) * sin_t[at, :]).astype(BF)
        vb[at, :] = wide[at, 2 * local_width : 3 * local_width].astype(BF)

    gather_forward(ag_o)
    scale = HEAD_DIM ** (-0.5)

    def head(ref, h, at=slice(None)):
        return ref[at, h * HEAD_DIM : (h + 1) * HEAD_DIM]

    block = 2 * rows

    @pl.loop(0, length // block)
    def _(r):
        at = pl.ds(pl.multiple_of(r * block, block), block)
        outs = []
        for h in range(heads):
            scores = nt(head(qk, h, at), head(qk, heads + h)) * scale
            peak = jnp.max(scores, axis=-1, keepdims=True)
            e = jnp.exp(scores - peak)
            probs = e / jnp.sum(e, axis=-1, keepdims=True)
            pbuf[h, at, :] = probs
            outs.append(nn(probs.astype(BF), head(vb, h)))
        att[at, :] = jnp.concatenate(outs, axis=1).astype(BF)

    gather_end(ag_o)

    rs_a = scatter_sum(0, att, wof[...].reshape(width, local_width))
    gather_forward(ag_i)
    inv_two = []
    sp2 = spread_open(x2)
    for p in range(PARTS):
        at = part_at(p)
        mixed[at, :] = tok[at, :].astype(F32) + scatter_end(rs_a, p)
        normed_two, inv = norm(mixed[at, :])
        inv_two.append(inv)
        xh2[at, :] = normed_two
        x2[mp, at, :] = (normed_two * gain_two).astype(BF)
        spread_start(sp2, p)
    gather_forward(ag_d)
    spread_forward(sp2)
    gather_end(ag_i)
    spread_end(sp2)
    wide[:, : 2 * units] = nn(
        x2[...].reshape(length, width), wif[...].reshape(width, 2 * units)
    )
    turn(x2, xt2)
    gather_end(ag_d)
    hgrad_buf[...] = nn(xc[...].reshape(length, width), wdf[...].reshape(width, units))

    @pl.loop(0, nmp)
    def _(r):
        at = chunk(r)
        u = wide[at, :units]
        gate = wide[at, units : 2 * units]
        cdf = 0.5 * (1.0 + erf(u * 0.7071067811865476))
        act = u * cdf
        slope = cdf + u * jnp.exp(-0.5 * u * u) * 0.3989422804014327
        hid[at, :] = (act * gate).astype(BF)
        hgrad = hgrad_buf[at, :]
        lg[at, :] = jnp.concatenate([hgrad * gate * slope, hgrad * act], axis=1).astype(BF)

    rs_g = scatter_sum(1, lg, wif[...].reshape(width, 2 * units))
    g_d = grad_start(xtc, hid[...], gsd, grd, gwd)
    g_i = grad_start(xt2, lg[...], gsi, gri, gwi)
    grad_own(xtc, hid[...], gwd)
    sp3 = spread_open(x3)
    for p in range(PARTS):
        at = part_at(p)
        back_two = norm_back(scatter_end(rs_g, p), xh2[at, :], inv_two[p], gain_two)
        mgrad[at, :] = cot[at, :].astype(F32) + back_two
        x3[mp, at, :] = mgrad[at, :].astype(BF)
        spread_start(sp3, p)
    grad_own(xt2, lg[...], gwi)
    rs_o = scatter_sum(3, hid, wdf[...].reshape(width, units))
    spread_forward(sp3)
    g_d = grad_middle(g_d, gzd, gyd)
    spread_end(sp3)
    turn(x3, xt3)
    g_o = grad_start(xt3, att[...], gso, gro, gwo)

    dks[...] = jnp.zeros_like(dks)
    dvs[...] = jnp.zeros_like(dvs)

    gatt[...] = nn(
        x3[...].reshape(length, width), wof[...].reshape(width, local_width)
    ).astype(BF)

    for r in range(length // block):
        at = pl.ds(r * block, block)
        agrad = gatt[at, :]
        out_rows = att[at, :]
        for h in range(heads):
            g = agrad[:, h * HEAD_DIM : (h + 1) * HEAD_DIM]
            o = out_rows[:, h * HEAD_DIM : (h + 1) * HEAD_DIM]
            probs = pbuf[h, at, :]
            dvs[h] += tn(probs.astype(BF), g)
            dprobs = nt(g, head(vb, h))
            delta = jnp.sum(g.astype(F32) * o.astype(F32), axis=-1, keepdims=True)
            ds = (probs * (dprobs - delta) * scale).astype(BF)
            dqs[h, at, :] = nn(ds, head(qk, heads + h))
            dks[h] += tn(ds, head(qk, h, at))
        if r == 0:
            g_i = grad_middle(g_i, gzi, gyi)

    grad_own(xt3, att[...], gwo)
    g_o = grad_middle(g_o, gzo, gyo)

    @pl.loop(0, nmp)
    def _(r):
        at = chunk(r)
        both = jnp.concatenate(
            [dqs[h, at, :] for h in range(heads)] + [dks[h, at, :] for h in range(heads)], axis=1
        )
        for t in tiles(2 * local_width // 128):
            u = both[:, t]
            pg[at, t] = (u * cos_t[at, :] - swap_halves(u) * sin_t[at, :]).astype(BF)
        pg[at, 2 * local_width :] = jnp.concatenate(
            [dvs[h, at, :] for h in range(heads)], axis=1
        ).astype(BF)

    g_q = grad_start(xt1, pg[...], gsq, grq, gwq)

    rs_f = scatter_sum(2, pg, wqf[...].reshape(width, 3 * local_width))
    grad_own(xt1, pg[...], gwq)
    g_q = grad_middle(g_q, gzq, gyq)
    for p in range(PARTS):
        at = part_at(p)
        own_inv = inv_one[p * part_rows : (p + 1) * part_rows]
        back_one = norm_back(scatter_end(rs_f, p), xh1[at, :], own_inv, gain_one)
        tg_o[at, :] = mgrad[at, :] + back_one
        out_o[at, :] = mixed[at, :] + scatter_end(rs_o, p)
    dd_o[...] = flip(grad_end(g_d))
    in_grad = grad_end(g_i)
    for i in range(2):
        di_o[:, i, :] = in_grad[:, i * units : (i + 1) * units]
    sum_two = jnp.sum(in_grad * wi[...].astype(F32), axis=-1, keepdims=True)
    do_o[...] = flip(grad_end(g_o))
    qkv_grad = grad_end(g_q)
    sum_one = jnp.sum(qkv_grad * wq[...].astype(F32), axis=-1, keepdims=True)
    lane = lax.broadcasted_iota(jnp.int32, (shard, 128), 1)
    sums = jnp.where(lane < 1, sum_one / column(gain_a), sum_two / column(gain_b))
    ggs[...] = flip(sums)[:8]
    gain_sems = [slot() for _ in range(3)]
    for k, other in enumerate((ypeer, mate, diag)):
        put(ggs, ggr.at[k], gain_sems[k], at_mp(other))
    for i in range(3):
        dq_o[i] = qkv_grad[:, i * local_width : (i + 1) * local_width]
    total = ggs[...]
    for k in range(3):
        got(ggr.at[k], gain_sems[k])
        total = total + ggr[k]
    ga_o[...] = total[0:1]
    gb_o[...] = total[1:2]
    for copy in sends:
        copy.wait_send()


def settle_kernel(*refs):
    count = len(refs) // 2
    for src, dst in zip(refs[:count], refs[count:]):
        dst[...] = src[...]


def fused_shards(tokens, cotangent, attn_gain, w_qkv, w_attn_out, mlp_gain, w_in, w_mlp_out):
    ndp = lax.axis_size("dp")
    nmp = lax.axis_size("mp")
    rows, width = tokens.shape
    shard = w_qkv.shape[0]
    lw = w_qkv.shape[2]
    units = w_in.shape[2]
    heads = lw // HEAD_DIM
    length = rows * nmp
    na = ndp // PAIR
    half = HEAD_DIM // 2
    freqs = rope_base ** (-(np.arange(half, dtype=np.float32) * np.float32(2.0) / HEAD_DIM))
    angles = np.arange(length, dtype=np.float32)[:, None] * freqs.astype(np.float32)[None, :]
    cos_t = np.tile(np.cos(angles).astype(np.float32), (1, 128 // half))
    sin = np.sin(angles).astype(np.float32)
    sin_t = np.tile(np.concatenate([-sin, sin], axis=1), (1, 128 // HEAD_DIM))

    def buf(shape, dtype=BF):
        return pltpu.VMEM(shape, dtype)

    def grad_bufs(cols):
        return [
            buf((na, shard, cols)), buf((na, shard, cols)), buf((na, shard, cols)),
            buf((na, shard, cols)), buf((na, shard, cols), F32),
        ]

    nsem = ndp + 16 * na + 4 * (3 * PARTS) + 4 * (2 * PARTS + 1) + 8
    scratch = [
        buf((1, 2 * width), F32), buf((shard, 3 * lw)), buf((shard, lw)),
        buf((shard, 2 * units)), buf((shard, units)),
        buf((ndp, 1, 2 * width), F32),
        buf((ndp, shard, 3 * lw)), buf((ndp, shard, lw)),
        buf((ndp, shard, 2 * units)), buf((ndp, shard, units)),
        *[buf((nmp, rows, width)) for _ in range(4)],
        *[buf((na, PAIR, shard, length)) for _ in range(4)],
        buf((length, 2 * lw)), buf((length, lw)), buf((length, lw)),
        buf((heads, length, length), F32), buf((length, units)),
        buf((length, max(3 * lw, 2 * units)), F32), buf((length, units), F32),
        buf((length, 2 * units)), buf((length, 3 * lw)), buf((length, lw)),
        *[buf((heads, length, HEAD_DIM), F32) for _ in range(3)],
        *[buf((rows, width), F32) for _ in range(4)],
        buf((4, 2, rows, width)), buf((4, 2, rows, width)),
        buf((4, rows, width)), buf((4, rows, width)), buf((4, 2, rows, width), F32),
        *grad_bufs(3 * lw), *grad_bufs(lw), *grad_bufs(2 * units), *grad_bufs(units),
        buf((8, shard), F32), buf((3, 8, shard), F32),
        pltpu.SemaphoreType.DMA((nsem,)), pltpu.SemaphoreType.DMA((nsem,)),
    ]
    vmem = pl.BlockSpec(memory_space=pltpu.VMEM)
    shapes = [
        (rows, width), (rows, width), (1, shard), (1, shard), (3, shard, lw), (lw, shard),
        (shard, 2, units), (units, shard),
    ]
    out, tg, ga, gb, dq, do, di, dd = pl.pallas_call(
        functools.partial(layer_kernel, ndp, heads),
        out_shape=[jax.ShapeDtypeStruct(s, F32) for s in shapes],
        in_specs=[vmem] * 10,
        out_specs=[vmem] * 8,
        scratch_shapes=scratch,
        compiler_params=pltpu.CompilerParams(
            collective_id=0, has_side_effects=True, vmem_limit_bytes=60 * 1024 * 1024
        ),
    )(
        tokens, cotangent, attn_gain.reshape(1, shard), mlp_gain.reshape(1, shard),
        w_qkv.transpose(1, 0, 2), w_attn_out, w_in, w_mlp_out,
        jnp.asarray(cos_t), jnp.asarray(sin_t),
    )
    out, tg, ga, gb, dq, do, di, dd = pl.pallas_call(
        settle_kernel,
        out_shape=[jax.ShapeDtypeStruct(s, F32) for s in shapes],
        in_specs=[vmem] * 8,
        out_specs=[vmem] * 8,
    )(out, tg, ga, gb, dq, do, di, dd)
    return (
        out, tg, ga.reshape(shard), dq.transpose(1, 0, 2), do, gb.reshape(shard), di, dd,
    )


def choose(tokens, cotangent, attn_gain, w_qkv, w_attn_out, mlp_gain, w_in, w_mlp_out):
    ndp = lax.axis_size("dp")
    shard = w_qkv.shape[0]
    fits = (
        lax.axis_size("mp") == 4
        and ndp % PAIR == 0
        and shard % 16 == 0
        and shard <= 128
        and w_mlp_out.shape[1] == shard
        and tokens.shape[0] % 128 == 0
        and tokens.shape[0] <= 128
        and 2 * w_qkv.shape[2] % 128 == 0
    )
    form = fused_shards if fits else shards
    return form(tokens, cotangent, attn_gain, w_qkv, w_attn_out, mlp_gain, w_in, w_mlp_out)


def solution(mesh):
    in_specs = (
        P(("dp", "mp"), None),
        P(("dp", "mp"), None),
        P("dp"),
        P("dp", None, "mp"),
        P("mp", "dp"),
        P("dp"),
        P("dp", None, "mp"),
        P("mp", "dp"),
    )
    out_specs = (
        P(("dp", "mp"), None),
        P(("dp", "mp"), None),
        P("dp"),
        P("dp", None, "mp"),
        P("mp", "dp"),
        P("dp"),
        P("dp", None, "mp"),
        P("mp", "dp"),
    )
    return jax.shard_map(choose, mesh=mesh, in_specs=in_specs, out_specs=out_specs, check_vma=False)
```
